32 devices in a mesh: ops: 8 (over z, x), sec: 4 (over y, core).
Axes of the slice: x: 2, y: 2, z: 4, core: 2. Of those that a mesh axis runs over, the one named last changes fastest.
Arguments:
- wave_in: bfloat16 [4096, 4096], P('sec', 'ops'), may hold values from -16 to 16
- row_energy: float32 [4096], P('sec'), may hold values from 1 to 4
- row_operators: bfloat16 [32, 4096, 512], P('ops', 'sec'), may hold values from -0.25 to 0.25
- column_operators: bfloat16 [32, 512, 512], P('ops'), may hold values from -0.52734375 to 0.52734375
- term_count: int32 [8], P('ops'), may hold values from 1 to 4, 12 in all
- source: int32 [32], P('ops'), may hold values from 0 to 7
- target: int32 [32], P('ops'), may hold values from 0 to 7
Outputs:
- wave_next: float32 [4096, 4096], P('sec', 'ops')
- renormalized: float32 [32, 4096, 512], P('ops', 'sec')
- energy: float32 [], replicated
The draws below stay inside these ranges and needn't reach their ends.
Inputs may be any that keep to these rules, and one draw needn't show every extreme that they name: `term_count`: the counts sum to 12, and some index of ops holds exactly 4 terms.
All inputs are finite; a program needn't handle non-finite values. No bound on the sum of `term_count` on one device may be relied on, other than what follows from the above.
Results may differ from the reference program's by a relative error of at most 0.0095.
Values may be sent and summed in bfloat16 or wider, within the bound.
No kernel may reach another device: no remote copies, remote signals or barrier semaphores. Data moves between devices by JAX's collectives and lax.ppermute only.
A program may use at most 128 MiB of HBM per device.

```python
import math
import jax
import jax.numpy as jnp
import numpy as np
from jax import lax

SEC = 512
SECTORS = 8
COL_SECTORS = 8
SLOTS = 4
NS_STEPS = 2
ROWS = 4096
COLS = 4096
TERMS = 12
N_OPS = 8


def draw_wave_in(key, part):
    noise_key = jax.random.fold_in(key, 11)
    scale_key = jax.random.fold_in(key, 12)
    row_key = jax.random.fold_in(key, 13)
    col_key = jax.random.fold_in(key, 14)
    mixing_key = jax.random.fold_in(key, 15)
    signal_key = jax.random.fold_in(key, 16)
    weight_key = jax.random.fold_in(key, 17)
    order_key = jax.random.fold_in(key, 18)
    mode_count = SEC // 8
    order = jax.random.permutation(order_key, COL_SECTORS).astype(jnp.int32)
    column = jnp.arange(COLS, dtype=jnp.int32)
    ranked = order[column // SEC] * SEC + column % SEC
    position = ranked.astype(jnp.float32) / COLS
    rough = jax.random.uniform(scale_key, (COLS,), jnp.float32, jnp.log(0.75), jnp.log(1.33))
    row_common = jax.random.normal(row_key, (ROWS, 1), jnp.float32)
    col_common = jax.random.normal(col_key, (1, COLS), jnp.float32)
    mixing = jax.random.normal(mixing_key, (SECTORS, SEC, mode_count), jnp.float32)
    signal = jax.random.normal(signal_key, (SECTORS, mode_count, COLS), jnp.float32)
    weights = jnp.exp(jax.random.uniform(weight_key, (SECTORS, 1, mode_count), jnp.float32, jnp.log(0.3), jnp.log(0.5)))
    modal = jnp.einsum('sik,skc->sic', mixing * weights, signal)
    total = 1.0 + jnp.sum(weights * weights, axis=(1, 2))
    noise = jax.random.normal(noise_key, (SECTORS, SEC, COLS), jnp.float32)
    col_scale = jnp.exp(jnp.log(3.0) * position + rough)
    strength = position
    mixed = ((noise + modal) / jnp.sqrt(total)[:, None, None]).reshape(ROWS, COLS)
    values = col_scale[None, :] * (mixed + strength[None, :] * row_common * col_common)
    return jnp.clip(values, -16.0, 16.0).astype(jnp.bfloat16)


def place_ends(entries, rng, smallest, high):
    longest = entries.shape.index(max(entries.shape))
    spots = []
    for shift in (0, 1):
        where = [jax.random.randint(jax.random.fold_in(rng, axis), (), 0, length) for axis, length in enumerate(entries.shape)]
        where[longest] = (where[longest] + shift) % entries.shape[longest]
        spots.append(tuple(where))
    return entries.at[spots[0]].set(smallest).at[spots[1]].set(high)


def block_scale(key, dims, pieces, least, high):
    loudness, own = 1.0, jax.random.fold_in(key, 6)
    for axis_at, parts in pieces:
        heights = jnp.exp(jax.random.uniform(jax.random.fold_in(own, axis_at), (parts,), jnp.float32, least / len(pieces), high / len(pieces)))
        loudness = loudness * jnp.repeat(heights, dims[axis_at] // parts).reshape([-1 if axis == axis_at else 1 for axis in range(len(dims))])
    return loudness


def split_up(count, total, limit, lean):
    loads = [(1 << 20) // math.isqrt(rank ** lean) + 1 for rank in range(2, count + 1)]
    spare, holding = total - limit - (count - 1), [1] * (count - 1)
    while spare > 0:
        free = [i for i in range(count - 1) if holding[i] < limit]
        whole, budget = sum([loads[i] for i in free]), spare
        for i in free:
            more = min(limit - holding[i], max(1, budget * loads[i] // whole), spare)
            holding[i] = holding[i] + more
            spare = spare - more
    return np.array([limit] + holding)


def uneven_parts(own_key, amount, total, reach, skew):
    if amount == 2:
        one = jax.random.randint(own_key, (), max(1, total - reach), min(reach, total - 1) + 1)
        return jnp.stack([one, total - one])
    lengths = jnp.asarray(split_up(amount, total, reach, skew), jnp.int32)
    twos = (amount - 1) // 2
    giver, receiver = lengths[1:1 + 2 * twos:2], lengths[2:2 + 2 * twos:2]
    room = jnp.minimum(giver - 1, reach - receiver)
    shifted = jax.random.randint(jax.random.fold_in(own_key, 1), (twos,), 0, 1 << 20) % (room + 1)
    lengths = lengths.at[1:1 + 2 * twos:2].set(giver - shifted).at[2:2 + 2 * twos:2].set(receiver + shifted)
    return lengths[jax.random.permutation(jax.random.fold_in(own_key, 2), amount)]


def normal_values(own_key, shape, width, most, cuts=(), kind=jnp.bfloat16):
    factor_of = block_scale(own_key, shape, cuts, -0.22, 0.18) if cuts else 1.0
    values = jax.random.normal(own_key, shape, jnp.float32) * width * factor_of
    return jnp.minimum(jnp.maximum(values, -most), most).astype(kind)


def setup_inputs(seed: int = 0) -> dict:
    streams_of = jax.random.split(jax.random.key(seed), 8)
    wave_in = draw_wave_in(jax.random.fold_in(streams_of[7], 71), 0)
    row_energy = jnp.clip(1.0 + 3.0 * jax.random.uniform(streams_of[1], (ROWS,), jnp.float32) ** block_scale(streams_of[1], (ROWS,), ((0, 4),), -0.2, 0.2), 1.0, 4.0)
    row_operators = normal_values(streams_of[2], (SLOTS * N_OPS, ROWS, SEC), SEC ** -0.5, 0.25, ((0, 8), (1, 4)))
    column_operators = normal_values(streams_of[3], (SLOTS * N_OPS, SEC, SEC), (2.0 / SEC ** 0.5), 0.52734375, ((0, 8),))
    term_count = uneven_parts(streams_of[4], N_OPS, TERMS, SLOTS, 2).astype(jnp.int32)
    source = place_ends(jax.random.randint(streams_of[5], (SLOTS * N_OPS,), 0, COL_SECTORS), jax.random.fold_in(streams_of[5], 1), 0, COL_SECTORS - 1).astype(jnp.int32)
    target = place_ends(jax.random.randint(streams_of[6], (SLOTS * N_OPS,), 0, COL_SECTORS), jax.random.fold_in(streams_of[6], 1), 0, COL_SECTORS - 1).astype(jnp.int32)
    return {"wave_in": wave_in, "row_energy": row_energy, "row_operators": row_operators, "column_operators": column_operators, "term_count": term_count, "source": source, "target": target}


def precise(spec, first, second):
    return jnp.einsum(spec, first, second, precision=lax.Precision.HIGHEST)

def gram_of(first, second):
    return precise('sic,sjc->sij', first, second) / COLS

def inverse_root(gram_matrix):
    scaling = jnp.sqrt(lax.optimization_barrier(jnp.sum(gram_matrix * gram_matrix, axis=(1, 2), keepdims=True)) + 1e-06)
    identity = jnp.broadcast_to(jnp.eye(gram_matrix.shape[-1], dtype=jnp.float32), gram_matrix.shape)
    iterate = gram_matrix / scaling
    inverse = identity
    for repeat in range(NS_STEPS):
        middle = 1.5 * identity - 0.5 * precise('sij,sjk->sik', inverse, iterate)
        iterate = precise('sij,sjk->sik', iterate, middle)
        inverse = precise('sij,sjk->sik', middle, inverse)
    return (inverse, scaling)

def reference(wave_in, row_energy, row_operators, column_operators, term_count, source, target):
    amplitude = wave_in.astype(jnp.float32)

    def add_term(partial_value, term_slot):
        source_col = source[term_slot] * SEC
        target_col = target[term_slot] * SEC
        sector_cols = lax.dynamic_slice_in_dim(wave_in, source_col, SEC, 1).reshape(SECTORS, SEC, SEC).astype(jnp.float32)
        row_blocks = row_operators[term_slot].reshape(SECTORS, SEC, SEC).astype(jnp.float32)
        inner_prod = precise('sij,sjk->sik', row_blocks, sector_cols).astype(jnp.bfloat16)
        contribution = jnp.dot(inner_prod.reshape(ROWS, SEC), column_operators[term_slot], preferred_element_type=jnp.float32)
        existing = lax.dynamic_slice_in_dim(partial_value, target_col, SEC, 1)
        return lax.dynamic_update_slice_in_dim(partial_value, existing + contribution, target_col, 1)

    def per_device(running, device):

        def per_slot(partial_value, offset):
            term_slot = device * SLOTS + offset
            active = offset < term_count[device]
            updated = lax.cond(active, lambda carried: add_term(carried, term_slot), lambda carried: carried, partial_value)
            return (updated, None)
        partial_value, unused = lax.scan(per_slot, jnp.zeros((ROWS, COLS), jnp.float32), jnp.arange(SLOTS, dtype=jnp.int32))
        rounded = lax.optimization_barrier(partial_value.astype(jnp.bfloat16))
        return (running + rounded.astype(jnp.float32), None)
    summed, unused = lax.scan(per_device, jnp.zeros((ROWS, COLS), jnp.float32), jnp.arange(N_OPS, dtype=jnp.int32))
    applied = row_energy[:, None] * amplitude + summed
    energy = jnp.sum(amplitude * applied) / (ROWS * COLS)
    stepped = amplitude + 0.5 * (energy * amplitude - applied)
    stepped3 = stepped.reshape(SECTORS, SEC, COLS)
    gram_one = gram_of(stepped3, stepped3)
    root_one, scale_one = inverse_root(gram_one)
    basis_one = precise('sij,sjc->sic', root_one, stepped3) / jnp.sqrt(scale_one)
    gram_two = gram_of(basis_one, basis_one)
    root_two, scale_two = inverse_root(gram_two)
    wave_next = (precise('sij,sjc->sic', root_two, basis_one) / jnp.sqrt(scale_two)).reshape(ROWS, COLS)
    wave_half = wave_next.astype(jnp.bfloat16)

    def renorm(term_slot):
        active = term_slot % SLOTS < term_count[term_slot // SLOTS]

        def build_block(unused_arg):
            source_block = lax.dynamic_slice_in_dim(wave_half, source[term_slot] * SEC, SEC, 1).reshape(SECTORS, SEC, SEC).astype(jnp.float32)
            target_block = lax.dynamic_slice_in_dim(wave_half, target[term_slot] * SEC, SEC, 1).reshape(SECTORS, SEC, SEC).astype(jnp.float32)
            product = precise('sij,jk->sik', source_block, column_operators[term_slot].astype(jnp.float32)).astype(jnp.bfloat16)
            result = precise('sik,slk->sil', product.astype(jnp.float32), target_block) * SEC ** (-0.5)
            return result.reshape(ROWS, SEC)
        return lax.cond(active, build_block, lambda unused_arg: jnp.zeros((ROWS, SEC), jnp.float32), 0)
    renormalized = lax.map(renorm, jnp.arange(SLOTS * N_OPS, dtype=jnp.int32))
    return (wave_next, renormalized, energy)
```

```python
import functools

import jax
import jax.numpy as jnp
from jax import lax
from jax.experimental import pallas as pl
from jax.experimental.pallas import tpu as pltpu
from jax.sharding import PartitionSpec as P

SEC = 512
COLUMN_SECTORS = 8
PAIR = 2


def halves(value):
    high = value.astype(jnp.bfloat16)
    return high, (value - high.astype(jnp.float32)).astype(jnp.bfloat16)


def dot(first, second):
    return jnp.dot(first, second, preferred_element_type=jnp.float32)


def dot_transposed(first, second):
    return lax.dot_general(
        first, second, (((1,), (1,)), ((), ())), preferred_element_type=jnp.float32
    )


def dot_split(first, second):
    (first_high, first_low), (second_high, second_low) = first, second
    return dot(first_high, second_high) + (dot(first_high, second_low) + dot(first_low, second_high))


def dot_fine(first, second):
    return dot_split(halves(first), halves(second))


def term_kernel(chunk, slots, meta, rows_hbm, cols_hbm, *refs):
    count = meta[0]
    blocks, outs = refs[:COLUMN_SECTORS], refs[COLUMN_SECTORS : 2 * COLUMN_SECTORS]
    row_buf, col_buf, wave_buf, total, sems = refs[2 * COLUMN_SECTORS :]

    def row_copy(k):
        part = rows_hbm.at[k, pl.ds(chunk * SEC, SEC)]
        return pltpu.make_async_copy(part, row_buf.at[k], sems.at[0, k])

    def col_copy(k):
        return pltpu.make_async_copy(cols_hbm.at[k], col_buf.at[k], sems.at[1, k])

    def wave_copy(k, block):
        return pltpu.make_async_copy(block, wave_buf.at[k], sems.at[2, k])

    @pl.loop(0, count)
    def start(k):
        row_copy(k).start()
        col_copy(k).start()
        for index, block in enumerate(blocks):

            @pl.when(meta[1 + k] == index)
            def fetch(block=block):
                wave_copy(k, block).start()

    total[...] = jnp.zeros_like(total)

    @pl.loop(0, count)
    def compute(k):
        row_copy(k).wait()
        wave_copy(k, blocks[0]).wait()
        inner = dot(row_buf[k], wave_buf[k]).astype(jnp.bfloat16)
        col_copy(k).wait()
        place = meta[1 + slots + k]
        total[place] = total[place] + dot(inner, col_buf[k])

    for index, out in enumerate(outs):
        out[...] = total[index].astype(jnp.bfloat16)


def term_sums(chunk, meta, row_operators, column_operators, blocks):
    slots = row_operators.shape[0]
    anywhere = pl.BlockSpec(memory_space=pl.ANY)
    return pl.pallas_call(
        functools.partial(term_kernel, chunk, slots),
        out_shape=[jax.ShapeDtypeStruct((SEC, SEC), jnp.bfloat16)] * COLUMN_SECTORS,
        in_specs=[pl.BlockSpec(memory_space=pltpu.SMEM)] + [anywhere] * (2 + COLUMN_SECTORS),
        out_specs=[pl.BlockSpec(memory_space=pltpu.VMEM)] * COLUMN_SECTORS,
        scratch_shapes=[
            pltpu.VMEM((slots, SEC, SEC), jnp.bfloat16),
            pltpu.VMEM((slots, SEC, SEC), jnp.bfloat16),
            pltpu.VMEM((slots, SEC, SEC), jnp.bfloat16),
            pltpu.VMEM((COLUMN_SECTORS, SEC, SEC), jnp.float32),
            pltpu.SemaphoreType.DMA((3, slots)),
        ],
        cost_estimate=pl.CostEstimate(flops=8 * SEC**3, bytes_accessed=14 * SEC * SEC, transcendentals=0),
        name="term_sums",
    )(meta, row_operators, column_operators, *blocks)


def inverse_root(scaled):
    row = lax.broadcasted_iota(jnp.int32, scaled.shape, 0)
    col = lax.broadcasted_iota(jnp.int32, scaled.shape, 1)
    identity = jnp.where(row == col, 1.0, 0.0).astype(jnp.float32)
    square = dot_fine(scaled, scaled)
    high = dot_fine(0.0625 * square - 0.5625 * scaled, square)
    return 2.25 * identity - 2.4375 * scaled + 1.6875 * square + high


def scaling_of(gram):
    return jnp.sqrt(jnp.sum(gram * gram, keepdims=True) + 1e-6)


def finish_kernel(chunk, slots, width, cols, meta, energy, row_energy, own_wave, own_sum, cols_hbm, *refs):
    count = meta[0]
    n = COLUMN_SECTORS
    waves, sums = refs[:n], refs[n : 2 * n]
    rest = refs[2 * n :]
    if chunk:
        rest = rest[2:]
    next_hbm, table_hbm, wave_buf, sum_buf, col_buf, next_buf, out_buf, sems, out_sems, next_sem = rest

    def wave_copy(b):
        return pltpu.make_async_copy(waves[b], wave_buf.at[b], sems.at[0, b])

    def sum_copy(b):
        return pltpu.make_async_copy(sums[b], sum_buf.at[b], sems.at[1, b])

    def col_copy(k):
        return pltpu.make_async_copy(cols_hbm.at[k], col_buf.at[k], sems.at[2, k])

    def out_copy(k):
        part = table_hbm.at[k, pl.ds(chunk * SEC, SEC)]
        return pltpu.make_async_copy(out_buf.at[k], part, out_sems.at[k])

    next_copy = pltpu.make_async_copy(next_buf, next_hbm.at[pl.ds(chunk * SEC, SEC)], next_sem)

    for b in range(n):
        wave_copy(b).start()
        sum_copy(b).start()
    for k in range(slots):
        col_copy(k).start()
    scale = 1.0 + 0.5 * energy[0] - 0.5 * row_energy[...]

    @pl.loop(count, slots)
    def clear(k):
        out_buf[k] = jnp.zeros((SEC, SEC), jnp.float32)
        out_copy(k).start()

    def stepped(b):
        return scale * wave_buf[b].astype(jnp.float32) - 0.5 * sum_buf[b].astype(jnp.float32)

    gram = jnp.zeros((SEC, SEC), jnp.float32)
    for b in range(n):
        wave_copy(b).wait()
        sum_copy(b).wait()
        part = stepped(b).astype(jnp.bfloat16)
        gram = gram + dot_transposed(part, part)
    gram = gram / cols
    scale_one = scaling_of(gram)
    scaled = gram / scale_one
    root_one = inverse_root(scaled)
    gram_two = dot_fine(scaled, dot_fine(root_one, root_one))
    scale_two = scaling_of(gram_two)
    root_two = inverse_root(gram_two / scale_two)
    mixer = halves(dot_fine(root_two, root_one) / (jnp.sqrt(scale_one) * jnp.sqrt(scale_two)))

    own = scale * own_wave[...].astype(jnp.float32) - 0.5 * own_sum[...]
    next_buf[...] = dot_split(mixer, halves(own))
    next_copy.start()
    for k in range(slots):
        col_copy(k).wait()

    @pl.loop(0, count)
    def renormalize(k):
        source = dot_split(mixer, halves(stepped(meta[1 + k]))).astype(jnp.bfloat16)
        target = dot_split(mixer, halves(stepped(meta[1 + slots + k]))).astype(jnp.bfloat16)
        product = dot(source, col_buf[k]).astype(jnp.bfloat16)
        out_buf[k] = dot_transposed(product, target) * SEC ** (-0.5)
        out_copy(k).start()

    next_copy.wait()
    for k in range(slots):
        out_copy(k).wait()


def finish(chunk, rows, cols, meta, energy, row_energy, own_wave, own_sum, column_operators, waves, sums, earlier):
    slots = column_operators.shape[0]
    width = own_wave.shape[1]
    anywhere = pl.BlockSpec(memory_space=pl.ANY)
    vmem = pl.BlockSpec(memory_space=pltpu.VMEM)
    smem = pl.BlockSpec(memory_space=pltpu.SMEM)
    operands = [meta, energy, row_energy, own_wave, own_sum, column_operators, *waves, *sums, *earlier]
    fixed = 6 + 2 * COLUMN_SECTORS
    return pl.pallas_call(
        functools.partial(finish_kernel, chunk, slots, width, cols),
        out_shape=[
            jax.ShapeDtypeStruct((rows, width), jnp.float32),
            jax.ShapeDtypeStruct((slots, rows, SEC), jnp.float32),
        ],
        in_specs=[smem, smem, vmem, vmem, vmem] + [anywhere] * (len(operands) - 5),
        out_specs=[anywhere, anywhere],
        scratch_shapes=[
            pltpu.VMEM((COLUMN_SECTORS, SEC, SEC), jnp.bfloat16),
            pltpu.VMEM((COLUMN_SECTORS, SEC, SEC), jnp.bfloat16),
            pltpu.VMEM((slots, SEC, SEC), jnp.bfloat16),
            pltpu.VMEM((SEC, width), jnp.float32),
            pltpu.VMEM((slots, SEC, SEC), jnp.float32),
            pltpu.SemaphoreType.DMA((3, max(slots, COLUMN_SECTORS))),
            pltpu.SemaphoreType.DMA((slots,)),
            pltpu.SemaphoreType.DMA,
        ],
        input_output_aliases={fixed: 0, fixed + 1: 1} if earlier else {},
        cost_estimate=pl.CostEstimate(flops=100 * SEC**3, bytes_accessed=40 * SEC * SEC, transcendentals=0),
        name="finish",
    )(*operands)


class Line:
    def __init__(self, size):
        self.size = size
        self.length = size // PAIR
        self.place = lax.axis_index("ops")

    def permute(self, value, shift, cross):
        pairs = []
        for z in range(self.length):
            for x in range(PAIR):
                to = ((z + shift) % self.length) * PAIR + (x + cross) % PAIR
                pairs.append((z * PAIR + x, to))
        return lax.ppermute(value, "ops", pairs)

    def gather(self, block):
        direct = [block] + [self.permute(block, d, 0) for d in range(1, self.length)]
        out = []
        for value in direct:
            out += [value, self.permute(value, 0, 1)]
        return out

    def gathered_at(self, sector):
        away = (self.place // PAIR - sector // PAIR) % self.length
        return away * PAIR + (self.place + sector) % PAIR

    def scattered_at(self, sector):
        away = (sector // PAIR - self.place // PAIR) % self.length
        return away * PAIR + (self.place + sector) % PAIR

    def scatter(self, parts):
        total = None
        for d in range(self.length):
            other = self.permute(parts[PAIR * d + 1], 0, 1)
            both = parts[PAIR * d].astype(jnp.float32) + other.astype(jnp.float32)
            if d:
                both = self.permute(both.astype(jnp.bfloat16), d, 0).astype(jnp.float32)
            total = both if total is None else total + both
        return total


class Whole:
    def gather(self, block):
        everything = lax.all_gather(block, "ops", axis=1, tiled=True)
        return [everything[:, i * SEC : (i + 1) * SEC] for i in range(COLUMN_SECTORS)]

    def gathered_at(self, sector):
        return sector

    def scattered_at(self, sector):
        return sector

    def scatter(self, parts):
        joined = jnp.concatenate(parts, axis=1)
        return lax.psum_scatter(joined, "ops", scatter_dimension=1, tiled=True).astype(jnp.float32)


def sum_everywhere(value, sizes):
    for axis, size in sizes.items():
        if size & (size - 1):
            value = lax.psum(value, axis)
            continue
        step = 1
        while step < size:
            value = value + lax.ppermute(value, axis, [(i, i ^ step) for i in range(size)])
            step *= 2
    return value


def on_device(sizes, wave_in, row_energy, row_operators, column_operators, term_count, source, target):
    rows, width = wave_in.shape
    chunks = rows // SEC
    cols = width * sizes["ops"]
    entries = cols * rows * sizes["sec"]
    paired = width == SEC and sizes["ops"] % PAIR == 0 and sizes["ops"] == COLUMN_SECTORS
    links = Line(sizes["ops"]) if paired else Whole()

    def table(placed_source, placed_target):
        return jnp.concatenate([term_count, placed_source, placed_target]).astype(jnp.int32)

    sum_meta = table(links.gathered_at(source), links.scattered_at(target))
    end_meta = table(links.gathered_at(source), links.gathered_at(target))
    waves_own = [wave_in[i * SEC : (i + 1) * SEC] for i in range(chunks)]
    heights = [row_energy[i * SEC : (i + 1) * SEC][:, None] for i in range(chunks)]

    waves = [links.gather(block) for block in waves_own]
    sums_own = []
    for i in range(chunks):
        parts = term_sums(i, sum_meta, row_operators, column_operators, waves[i])
        sums_own.append(links.scatter(parts))
    numerator = jnp.zeros((), jnp.float32)
    for i in range(chunks):
        amplitude = waves_own[i].astype(jnp.float32)
        numerator = numerator + jnp.sum(amplitude * (heights[i] * amplitude + sums_own[i]))
    energy = sum_everywhere(jnp.full((8, 128), numerator), sizes)[0, 0] / entries
    sums = [links.gather(own.astype(jnp.bfloat16)) for own in sums_own]
    outs = ()
    for i in range(chunks):
        outs = finish(
            i, rows, cols, end_meta, energy[None], heights[i], waves_own[i], sums_own[i],
            column_operators, waves[i], sums[i], outs,
        )
    return (outs[0], outs[1], energy)


def solution(mesh):
    placed = (
        P("sec", "ops"),
        P("sec"),
        P("ops", "sec", None),
        P("ops", None, None),
        P("ops"),
        P("ops"),
        P("ops"),
    )
    return jax.shard_map(
        functools.partial(on_device, dict(mesh.shape)),
        mesh=mesh,
        in_specs=placed,
        out_specs=(P("sec", "ops"), P("ops", "sec", None), P()),
        check_vma=False,
    )
```

```python
import functools

import jax
import jax.numpy as jnp
from jax import lax
from jax.experimental import pallas as pl
from jax.experimental.pallas import tpu as pltpu
from jax.sharding import PartitionSpec as P

SEC = 512
COLUMN_SECTORS = 8
HALVES = 2
HALF = SEC // HALVES


def halves(value):
    high = value.astype(jnp.bfloat16)
    return high, (value - high.astype(jnp.float32)).astype(jnp.bfloat16)


def dot(first, second):
    return jnp.dot(first, second, preferred_element_type=jnp.float32)


def dot_transposed(first, second):
    return lax.dot_general(
        first, second, (((1,), (1,)), ((), ())), preferred_element_type=jnp.float32
    )


def dot_split(first, second):
    (first_high, first_low), (second_high, second_low) = first, second
    return dot(first_high, second_high) + (dot(first_high, second_low) + dot(first_low, second_high))


def dot_fine(first, second):
    return dot_split(halves(first), halves(second))


def term_kernel(chunk, slots, meta, rows_hbm, cols_hbm, *refs):
    count = meta[0]
    pieces = COLUMN_SECTORS * HALVES
    blocks, outs = refs[:pieces], refs[pieces : 2 * pieces]
    energy_out, row_buf, col_buf, wave_buf, target_buf, total, sems = refs[2 * pieces :]

    def row_copy(k):
        part = rows_hbm.at[k, pl.ds(chunk * SEC, SEC)]
        return pltpu.make_async_copy(part, row_buf.at[k], sems.at[0, k])

    def col_copy(k):
        return pltpu.make_async_copy(cols_hbm.at[k], col_buf.at[k], sems.at[1, k])

    def wave_copy(k, piece, half):
        return pltpu.make_async_copy(blocks[piece], wave_buf.at[k, pl.ds(half * HALF, HALF)], sems.at[2 + half, k])

    def target_copy(k, piece, half):
        return pltpu.make_async_copy(blocks[piece], target_buf.at[k, pl.ds(half * HALF, HALF)], sems.at[2 + HALVES + half, k])

    @pl.loop(0, count)
    def start(k):
        row_copy(k).start()
        for index in range(COLUMN_SECTORS):

            @pl.when(meta[1 + k] == index)
            def fetch(index=index):
                for half in range(HALVES):
                    wave_copy(k, index * HALVES + half, half).start()

        col_copy(k).start()
        for index in range(COLUMN_SECTORS):

            @pl.when(meta[1 + 2 * slots + k] == index)
            def fetch_target(index=index):
                for half in range(HALVES):
                    target_copy(k, index * HALVES + half, half).start()

    total[...] = jnp.zeros_like(total)
    energy_out[...] = jnp.zeros_like(energy_out)

    @pl.loop(0, count)
    def compute(k):
        row_copy(k).wait()
        for half in range(HALVES):
            wave_copy(k, half, half).wait()
        inner = dot(row_buf[k], wave_buf[k]).astype(jnp.bfloat16)
        col_copy(k).wait()
        place = meta[1 + slots + k]
        contribution = dot(inner, col_buf[k])
        total[place] = total[place] + contribution
        for half in range(HALVES):
            target_copy(k, half, half).wait()
        overlap = target_buf[k].astype(jnp.float32) * contribution
        energy_out[...] += jnp.sum(overlap, axis=0, keepdims=True)

    for index in range(COLUMN_SECTORS):
        for half in range(HALVES):
            outs[index * HALVES + half][...] = total[index, pl.ds(half * HALF, HALF)].astype(jnp.bfloat16)


def term_sums(chunk, meta, row_operators, column_operators, blocks):
    slots = row_operators.shape[0]
    hbm = pl.BlockSpec(memory_space=pltpu.HBM)
    vmem = pl.BlockSpec(memory_space=pltpu.VMEM)
    pieces = COLUMN_SECTORS * HALVES
    buffer = pltpu.VMEM((slots, SEC, SEC), jnp.bfloat16)
    *parts, energy = pl.pallas_call(
        functools.partial(term_kernel, chunk, slots),
        out_shape=[jax.ShapeDtypeStruct((HALF, SEC), jnp.bfloat16)] * pieces
        + [jax.ShapeDtypeStruct((1, SEC), jnp.float32)],
        in_specs=[pl.BlockSpec(memory_space=pltpu.SMEM)] + [hbm] * (2 + pieces),
        out_specs=[vmem] * (pieces + 1),
        scratch_shapes=[
            buffer,
            buffer,
            buffer,
            buffer,
            pltpu.VMEM((COLUMN_SECTORS, SEC, SEC), jnp.float32),
            pltpu.SemaphoreType.DMA((2 + 2 * HALVES, slots)),
        ],
        cost_estimate=pl.CostEstimate(flops=8 * SEC**3, bytes_accessed=14 * SEC * SEC, transcendentals=0),
        name="term_sums",
    )(meta, row_operators, column_operators, *blocks)
    return parts, jnp.sum(energy)


def inverse_root(scaled):
    row = lax.broadcasted_iota(jnp.int32, scaled.shape, 0)
    col = lax.broadcasted_iota(jnp.int32, scaled.shape, 1)
    identity = jnp.where(row == col, 1.0, 0.0).astype(jnp.float32)
    square = dot_fine(scaled, scaled)
    high = dot_fine(0.0625 * square - 0.5625 * scaled, square)
    return 2.25 * identity - 2.4375 * scaled + 1.6875 * square + high


def scaling_of(gram):
    return jnp.sqrt(jnp.sum(gram * gram, keepdims=True) + 1e-6)


def finish_kernel(chunk, slots, width, cols, meta, energy, row_energy, own_wave, own_sum, cols_hbm, *refs):
    count = meta[0]
    n = COLUMN_SECTORS
    pieces = n * HALVES
    waves, sums = refs[:pieces], refs[pieces : 2 * pieces]
    rest = refs[2 * pieces :]
    if chunk:
        rest = rest[2:]
    next_hbm, table_hbm, wave_buf, sum_buf, col_buf, next_buf, out_buf, sems, out_sems, next_sem = rest

    def piece_copies(b):
        copies = []
        for half in range(HALVES):
            index, span = b * HALVES + half, pl.ds(half * HALF, HALF)
            copies.append(pltpu.make_async_copy(waves[index], wave_buf.at[b, span], sems.at[0, index]))
            copies.append(pltpu.make_async_copy(sums[index], sum_buf.at[b, span], sems.at[1, index]))
        return copies

    def col_copy(k):
        return pltpu.make_async_copy(cols_hbm.at[k], col_buf.at[k], sems.at[2, k])

    def out_copy(k):
        part = table_hbm.at[k, pl.ds(chunk * SEC, SEC)]
        return pltpu.make_async_copy(out_buf.at[k], part, out_sems.at[k])

    next_copy = pltpu.make_async_copy(next_buf, next_hbm.at[pl.ds(chunk * SEC, SEC)], next_sem)

    for b in range(n):
        for copy in piece_copies(b):
            copy.start()
    for k in range(slots):
        col_copy(k).start()
    scale = 1.0 + 0.5 * energy[0] - 0.5 * row_energy[...]

    @pl.loop(count, slots)
    def clear(k):
        out_buf[k] = jnp.zeros((SEC, SEC), jnp.float32)
        out_copy(k).start()

    def stepped(b):
        return scale * wave_buf[b].astype(jnp.float32) - 0.5 * sum_buf[b].astype(jnp.float32)

    gram = jnp.zeros((SEC, SEC), jnp.float32)
    for b in range(n):
        for copy in piece_copies(b):
            copy.wait()
        part = stepped(b).astype(jnp.bfloat16)
        gram = gram + dot_transposed(part, part)
    gram = gram / cols
    scale_one = scaling_of(gram)
    scaled = gram / scale_one
    root_one = inverse_root(scaled)
    gram_two = dot_fine(scaled, dot_fine(root_one, root_one))
    scale_two = scaling_of(gram_two)
    root_two = inverse_root(gram_two / scale_two)
    mixer = halves(dot_fine(root_two, root_one) / (jnp.sqrt(scale_one) * jnp.sqrt(scale_two)))

    own = scale * own_wave[...].astype(jnp.float32) - 0.5 * own_sum[...]
    next_buf[...] = dot_split(mixer, halves(own))
    next_copy.start()
    for k in range(slots):
        col_copy(k).wait()

    @pl.loop(0, count)
    def renormalize(k):
        source = dot_split(mixer, halves(stepped(meta[1 + k]))).astype(jnp.bfloat16)
        target = dot_split(mixer, halves(stepped(meta[1 + slots + k]))).astype(jnp.bfloat16)
        product = dot(source, col_buf[k]).astype(jnp.bfloat16)
        out_buf[k] = dot_transposed(product, target) * SEC ** (-0.5)
        out_copy(k).start()

    next_copy.wait()
    for k in range(slots):
        out_copy(k).wait()


def finish(chunk, rows, cols, meta, energy, row_energy, own_wave, own_sum, column_operators, waves, sums, earlier):
    slots = column_operators.shape[0]
    width = own_wave.shape[1]
    anywhere = pl.BlockSpec(memory_space=pltpu.HBM)
    vmem = pl.BlockSpec(memory_space=pltpu.VMEM)
    smem = pl.BlockSpec(memory_space=pltpu.SMEM)
    operands = [meta, energy, row_energy, own_wave, own_sum, column_operators, *waves, *sums, *earlier]
    fixed = 6 + 2 * COLUMN_SECTORS * HALVES
    return pl.pallas_call(
        functools.partial(finish_kernel, chunk, slots, width, cols),
        out_shape=[
            jax.ShapeDtypeStruct((rows, width), jnp.float32),
            jax.ShapeDtypeStruct((slots, rows, SEC), jnp.float32),
        ],
        in_specs=[smem, smem, vmem, vmem, vmem] + [anywhere] * (len(operands) - 5),
        out_specs=[anywhere, anywhere],
        scratch_shapes=[
            pltpu.VMEM((COLUMN_SECTORS, SEC, SEC), jnp.bfloat16),
            pltpu.VMEM((COLUMN_SECTORS, SEC, SEC), jnp.bfloat16),
            pltpu.VMEM((slots, SEC, SEC), jnp.bfloat16),
            pltpu.VMEM((SEC, width), jnp.float32),
            pltpu.VMEM((slots, SEC, SEC), jnp.float32),
            pltpu.SemaphoreType.DMA((3, max(slots, COLUMN_SECTORS * HALVES))),
            pltpu.SemaphoreType.DMA((slots,)),
            pltpu.SemaphoreType.DMA,
        ],
        input_output_aliases={fixed: 0, fixed + 1: 1} if earlier else {},
        cost_estimate=pl.CostEstimate(flops=100 * SEC**3, bytes_accessed=40 * SEC * SEC, transcendentals=0),
        name="finish",
    )(*operands)


LINE = 4
PAIR = 2
SWAP = ((0, 1), (1, 0), (2, 3), (3, 2))
MIDDLE = ((1, 2), (2, 1))
OUTWARD = ((1, 0), (2, 3))
INWARD = ((0, 1), (3, 2))


def along_line(value, moves):
    pairs = [(z * PAIR + x, to * PAIR + x) for z, to in moves for x in range(PAIR)]
    return lax.ppermute(value, "ops", pairs)


def across(value):
    return lax.ppermute(value, "ops", [(i, i ^ 1) for i in range(LINE * PAIR)])


def shifted(value, axis, size, shift, unit):
    pairs = [(i, (i // unit + shift) % (size // unit) * unit + i % unit) for i in range(size)]
    return lax.ppermute(value, axis, pairs)


def add(*values):
    total = values[0].astype(jnp.float32)
    for value in values[1:]:
        total = total + value.astype(jnp.float32)
    return total


def add_half(*values):
    return add(*values).astype(jnp.bfloat16)


def line(moves):
    return lambda value: along_line(value, moves)


def gather_stream(block, lag, burst, at_middle):
    held, crossed = [block], []
    got = {}
    step = 0
    while len(crossed) < LINE:
        sends = {}
        if step == 0:
            sends["swap"] = (line(SWAP), block)
            sends["middle"] = (line(MIDDLE), block)
        if step == 1:
            sends["outward"] = (line(OUTWARD), middle)
            sends["turn"] = (line(MIDDLE), swap)
        if step == 2:
            sends["last"] = (line(OUTWARD), turn)
        first = step - lag
        if 0 <= first < LINE:
            for index in range(first, LINE if first >= burst else first + 1):
                if index == len(crossed) + len([k for k in sends if k[0] == "x"]):
                    sends["x" + str(index)] = (across, held[index])
        got = yield sends
        if step == 0:
            swap, middle = got["swap"], got["middle"]
            held.append(swap)
        if step == 1:
            turn = got["turn"]
            held.append(jnp.where(at_middle, middle, got["outward"]))
        if step == 2:
            held.append(jnp.where(at_middle, turn, got["last"]))
        crossed += [got[key] for key in sorted(got) if key[0] == "x"]
        step += 1
    return [value for pair in zip(held, crossed) for value in pair]


def scatter_stream(parts):
    far = [parts[PAIR * e + 1] for e in range(LINE)]
    near = [parts[PAIR * e] for e in range(LINE)]
    extra, result = {}, None
    for blocks in (far, near):
        sends = {"first": (line(INWARD), blocks[3])}
        if blocks is near:
            sends["x"] = (across, result.astype(jnp.bfloat16))
        got = yield sends
        if blocks is near:
            extra = [got["x"]]
        turned = add_half(blocks[2], got["first"])
        got = yield {"turn": (line(MIDDLE), turned), "inward": (line(INWARD), blocks[2])}
        swap, middle = add_half(blocks[1], got["turn"]), add_half(blocks[3], got["inward"])
        got = yield {"swap": (line(SWAP), swap), "middle": (line(MIDDLE), middle)}
        result = add(blocks[0], got["swap"], got["middle"])
    return add(result, *extra)


def scatter_across_stream(parts):
    far = [parts[PAIR * e + 1] for e in range(LINE)]
    near = [parts[PAIR * e] for e in range(LINE)]
    both = {}
    for e in (3, 2, 1):
        got = yield {"x": (across, far[e])}
        both[e] = add_half(near[e], got["x"])
    got = yield {"x": (across, far[0]), "first": (line(INWARD), both[3])}
    own = add(near[0], got["x"])
    turned = add_half(both[2], got["first"])
    got = yield {"turn": (line(MIDDLE), turned), "inward": (line(INWARD), both[2])}
    swap, middle = add_half(both[1], got["turn"]), add_half(both[3], got["inward"])
    got = yield {"swap": (line(SWAP), swap), "middle": (line(MIDDLE), middle)}
    return add(own, got["swap"], got["middle"])


def share_stream(value, groups):
    size = LINE * PAIR
    got = yield {d: (lambda v, d=d: shifted(v, "sec", groups, d, 1), value) for d in range(1, groups)}
    value = add(value, *got.values())
    got = yield {1: (across, value)}
    value = add(value, got[1])
    got = yield {d: (lambda v, d=d: shifted(v, "ops", size, d, PAIR), value) for d in range(1, LINE)}
    return add(value, *got.values())


class Rounds:
    def __init__(self):
        self.streams, self.events, self.results = {}, {}, {}

    def add(self, name, turn, stream):
        self.streams[name] = [turn, stream, None]

    def at(self, turn, event):
        self.events[turn] = event

    def run(self, turns):
        history = []
        for turn in range(turns):
            if turn in self.events:
                self.events[turn]()
            sends = []
            for name in list(self.streams):
                due, stream, got = self.streams[name]
                if due != turn:
                    continue
                try:
                    wanted = stream.send(got)
                except StopIteration as end:
                    self.results[name] = end.value
                    del self.streams[name]
                    continue
                sends += [(name, key, move, value) for key, (move, value) in wanted.items()]
                self.streams[name] = [turn + 2, stream, {}]
            earlier = history[turn - 2] if turn >= 2 else []
            values = [value for *_, value in sends]
            if values and earlier:
                values, _ = lax.optimization_barrier((values, earlier))
            here = []
            for (name, key, move, _), value in zip(sends, values):
                arrived = move(value)
                self.streams[name][2][key] = arrived
                here.append(arrived)
            history.append(here)


def halves_of(value):
    return [value[i * HALF : (i + 1) * HALF] for i in range(value.shape[0] // HALF)]


def on_links(groups, waves_own, table, terms, diagonal, ending):
    place = lax.axis_index("ops")
    z = place // PAIR
    at_middle = jnp.logical_or(z == 1, z == 2)

    def gathered_at(sector):
        away = z ^ (sector // PAIR)
        turned = jnp.logical_and(at_middle, away >= 2)
        return jnp.where(turned, 5 - away, away) * PAIR + ((place ^ sector) & 1)

    def scattered_at(sector):
        return (z ^ (sector // PAIR)) * PAIR + ((place ^ sector) & 1)

    source, target = table
    sum_places = [gathered_at(source), scattered_at(target), gathered_at(target)]
    end_places = [gathered_at(source), gathered_at(target)]
    rounds = Rounds()
    kept, energies = {}, {}

    def both(name, chunk):
        return [rounds.results[name + str(chunk) + str(half)] for half in range(HALVES)]

    def start(name, turn, make):
        for half in range(HALVES):
            rounds.add(name + str(half), turn + half, make(half))

    def spread(stream, parts, burst):
        own = yield from stream(parts)
        gathered = yield from gather_stream(own.astype(jnp.bfloat16), 2, burst, at_middle)
        return own, gathered

    def sum_terms(chunk, turn, stream, burst):
        def event():
            kept[chunk] = [piece for pair in zip(*both("wave", chunk)) for piece in pair]
            parts, energies[chunk] = terms(chunk, sum_places, kept[chunk])
            start("sum" + str(chunk), turn, lambda half: spread(stream, parts[half::HALVES], burst))

        return event

    def share_energy():
        index = place * groups + lax.axis_index("sec")
        slot = lax.broadcasted_iota(jnp.int32, (8, 128), 0) * 128 + lax.broadcasted_iota(jnp.int32, (8, 128), 1)
        total = diagonal + energies[0] + energies[1]
        rounds.add("energy", 20, share_stream(jnp.where(slot == index, total, 0.0), groups))

    waves = halves_of(waves_own)
    start("wave0", 2, lambda half: gather_stream(waves[half], 0, LINE, at_middle))
    start("wave1", 8, lambda half: gather_stream(waves[HALVES + half], 1, LINE, at_middle))
    rounds.at(12, sum_terms(0, 12, scatter_stream, LINE))
    rounds.at(20, lambda: (sum_terms(1, 20, scatter_across_stream, 1)(), share_energy()))
    rounds.run(48)
    energy = jnp.sum(rounds.results["energy"])
    own, sums = [], []
    for chunk in range(2):
        (top, top_sums), (low, low_sums) = both("sum", chunk)
        own.append(jnp.concatenate([top, low], axis=0))
        sums.append([piece for pair in zip(top_sums, low_sums) for piece in pair])
    return ending(energy, end_places, own, [kept[0], kept[1]], sums)


def anywhere(chunks, waves_own, table, terms, diagonal, ending):
    source, target = table

    def pieces_of(block):
        return [half for i in range(COLUMN_SECTORS) for half in halves_of(block[:, i * SEC : (i + 1) * SEC])]

    def gather(block):
        return pieces_of(lax.all_gather(block, "ops", axis=1, tiled=True))

    waves, own, energy = [], [], diagonal
    for chunk in range(chunks):
        waves.append(gather(waves_own[chunk * SEC : (chunk + 1) * SEC]))
        parts, part_energy = terms(chunk, [source, target, target], waves[chunk])
        energy = energy + part_energy
        columns = [jnp.concatenate(parts[i * HALVES : (i + 1) * HALVES], axis=0) for i in range(COLUMN_SECTORS)]
        joined = jnp.concatenate(columns, axis=1)
        own.append(lax.psum_scatter(joined, "ops", scatter_dimension=1, tiled=True).astype(jnp.float32))
    energy = lax.psum(energy, ("ops", "sec"))
    sums = [gather(value.astype(jnp.bfloat16)) for value in own]
    return ending(energy, [source, target], own, waves, sums)


def on_device(sizes, wave_in, row_energy, row_operators, column_operators, term_count, source, target):
    rows, width = wave_in.shape
    chunks = rows // SEC
    cols = width * sizes["ops"]
    entries = cols * rows * sizes["sec"]

    def table(places):
        return jnp.concatenate([term_count, *places]).astype(jnp.int32)

    def terms(chunk, places, blocks):
        return term_sums(chunk, table(places), row_operators, column_operators, blocks)

    def ending(numerator, places, own, waves, sums):
        energy = numerator / entries
        outs = ()
        for i in range(chunks):
            span = slice(i * SEC, (i + 1) * SEC)
            outs = finish(
                i, rows, cols, table(places), energy[None], row_energy[span][:, None], wave_in[span], own[i],
                column_operators, waves[i], sums[i], outs,
            )
        return (outs[0], outs[1], energy)

    amplitude = wave_in.astype(jnp.float32)
    diagonal = jnp.sum(row_energy[:, None] * amplitude * amplitude)
    planned = sizes["ops"] == LINE * PAIR == COLUMN_SECTORS and width == SEC and chunks == 2
    if planned:
        return on_links(sizes["sec"], wave_in, (source, target), terms, diagonal, ending)
    return anywhere(chunks, wave_in, (source, target), terms, diagonal, ending)


def solution(mesh):
    placed = (
        P("sec", "ops"),
        P("sec"),
        P("ops", "sec", None),
        P("ops", None, None),
        P("ops"),
        P("ops"),
        P("ops"),
    )
    return jax.shard_map(
        functools.partial(on_device, dict(mesh.shape)),
        mesh=mesh,
        in_specs=placed,
        out_specs=(P("sec", "ops"), P("ops", "sec", None), P()),
        check_vma=False,
    )
```

```python
import functools

import jax
import jax.numpy as jnp
from jax import lax
from jax.experimental import pallas as pl
from jax.experimental.pallas import tpu as pltpu
from jax.sharding import PartitionSpec as P

SEC = 512
COLUMN_SECTORS = 8
HALVES = 2
HALF = SEC // HALVES


def halves(value):
    high = value.astype(jnp.bfloat16)
    return high, (value - high.astype(jnp.float32)).astype(jnp.bfloat16)


def dot(first, second):
    return jnp.dot(first, second, preferred_element_type=jnp.float32)


def dot_transposed(first, second):
    return lax.dot_general(
        first, second, (((1,), (1,)), ((), ())), preferred_element_type=jnp.float32
    )


def dot_split(first, second):
    (first_high, first_low), (second_high, second_low) = first, second
    return dot(first_high, second_high) + (dot(first_high, second_low) + dot(first_low, second_high))


def dot_fine(first, second):
    return dot_split(halves(first), halves(second))


def term_kernel(chunk, slots, meta, rows_hbm, cols_hbm, *refs):
    count = meta[0]
    pieces = COLUMN_SECTORS * HALVES
    blocks, outs = refs[:pieces], refs[pieces : 2 * pieces]
    energy_out, row_buf, col_buf, wave_buf, target_buf, total, sems = refs[2 * pieces :]

    def row_copy(k):
        part = rows_hbm.at[k, pl.ds(chunk * SEC, SEC)]
        return pltpu.make_async_copy(part, row_buf.at[k], sems.at[0, k])

    def col_copy(k):
        return pltpu.make_async_copy(cols_hbm.at[k], col_buf.at[k], sems.at[1, k])

    def wave_copy(k, piece, half):
        return pltpu.make_async_copy(blocks[piece], wave_buf.at[k, pl.ds(half * HALF, HALF)], sems.at[2 + half, k])

    def target_copy(k, piece, half):
        return pltpu.make_async_copy(blocks[piece], target_buf.at[k, pl.ds(half * HALF, HALF)], sems.at[2 + HALVES + half, k])

    @pl.loop(0, count)
    def start(k):
        row_copy(k).start()
        for index in range(COLUMN_SECTORS):

            @pl.when(meta[1 + k] == index)
            def fetch(index=index):
                for half in range(HALVES):
                    wave_copy(k, index * HALVES + half, half).start()

        col_copy(k).start()
        for index in range(COLUMN_SECTORS):

            @pl.when(meta[1 + 2 * slots + k] == index)
            def fetch_target(index=index):
                for half in range(HALVES):
                    target_copy(k, index * HALVES + half, half).start()

    total[...] = jnp.zeros_like(total)
    energy_out[...] = jnp.zeros_like(energy_out)

    @pl.loop(0, count)
    def compute(k):
        row_copy(k).wait()
        for half in range(HALVES):
            wave_copy(k, half, half).wait()
        inner = dot(row_buf[k], wave_buf[k]).astype(jnp.bfloat16)
        col_copy(k).wait()
        place = meta[1 + slots + k]
        contribution = dot(inner, col_buf[k])
        total[place] = total[place] + contribution
        for half in range(HALVES):
            target_copy(k, half, half).wait()
        overlap = target_buf[k].astype(jnp.float32) * contribution
        energy_out[...] += jnp.sum(overlap, axis=0, keepdims=True)

    for index in range(COLUMN_SECTORS):
        for half in range(HALVES):
            outs[index * HALVES + half][...] = total[index, pl.ds(half * HALF, HALF)].astype(jnp.bfloat16)


def term_sums(chunk, meta, row_operators, column_operators, blocks):
    slots = row_operators.shape[0]
    hbm = pl.BlockSpec(memory_space=pltpu.HBM)
    vmem = pl.BlockSpec(memory_space=pltpu.VMEM)
    pieces = COLUMN_SECTORS * HALVES
    buffer = pltpu.VMEM((slots, SEC, SEC), jnp.bfloat16)
    *parts, energy = pl.pallas_call(
        functools.partial(term_kernel, chunk, slots),
        out_shape=[jax.ShapeDtypeStruct((HALF, SEC), jnp.bfloat16)] * pieces
        + [jax.ShapeDtypeStruct((1, SEC), jnp.float32)],
        in_specs=[pl.BlockSpec(memory_space=pltpu.SMEM)] + [hbm] * (2 + pieces),
        out_specs=[vmem] * (pieces + 1),
        scratch_shapes=[
            buffer,
            buffer,
            buffer,
            buffer,
            pltpu.VMEM((COLUMN_SECTORS, SEC, SEC), jnp.float32),
            pltpu.SemaphoreType.DMA((2 + 2 * HALVES, slots)),
        ],
        cost_estimate=pl.CostEstimate(flops=8 * SEC**3, bytes_accessed=14 * SEC * SEC, transcendentals=0),
        name="term_sums",
    )(meta, row_operators, column_operators, *blocks)
    return parts, jnp.sum(energy)


def scaling_of(gram):
    return jnp.sqrt(jnp.sum(gram * gram, keepdims=True) + 1e-6)


def finish_kernel(chunk, slots, cols, meta, energy, row_energy, wave_hbm, top_sum, low_sum, cols_hbm, *refs):
    count = meta[0]
    pieces = COLUMN_SECTORS * HALVES
    waves, sums = refs[:pieces], refs[pieces : 2 * pieces]
    rest = refs[2 * pieces :]
    if chunk:
        rest = rest[2:]
    next_hbm, table_hbm, wave_buf, sum_buf, col_buf, own_buf, next_buf, out_buf = rest[:8]
    gram_buf, root_buf, high_buf, low_buf, side_buf, factor_buf, sems, out_sems, own_sems = rest[8:]
    span = pl.ds(chunk * SEC, SEC)

    def piece_copies(b, source):
        copies = []
        for half in range(HALVES):
            index, part = source * HALVES + half, pl.ds(half * HALF, HALF)
            place = b * HALVES + half
            copies.append(pltpu.make_async_copy(waves[index], wave_buf.at[b, part], sems.at[0, place]))
            copies.append(pltpu.make_async_copy(sums[index], sum_buf.at[b, part], sems.at[1, place]))
        return copies

    def col_copy(k):
        return pltpu.make_async_copy(cols_hbm.at[k], col_buf.at[k], sems.at[2, k])

    def out_copy(k):
        return pltpu.make_async_copy(out_buf.at[k], table_hbm.at[k, span], out_sems.at[k])

    own_copy = pltpu.make_async_copy(wave_hbm.at[span], own_buf, own_sems.at[0])
    next_copy = pltpu.make_async_copy(next_buf, next_hbm.at[span], own_sems.at[1])

    for b in range(COLUMN_SECTORS):
        for copy in piece_copies(b, b):
            copy.start()
    own_copy.start()
    for k in range(slots):
        col_copy(k).start()
    scale = 1.0 + 0.5 * energy[0] - 0.5 * row_energy[span, :]

    @pl.loop(count, slots)
    def clear(k):
        out_buf[k] = jnp.zeros((SEC, SEC), jnp.float32)
        out_copy(k).start()

    def stepped(b):
        return scale * wave_buf[b].astype(jnp.float32) - 0.5 * sum_buf[b].astype(jnp.float32)

    gram_buf[...] = jnp.zeros_like(gram_buf)

    @pl.loop(0, COLUMN_SECTORS)
    def accumulate(b):
        for copy in piece_copies(b, 0):
            copy.wait()
        part = stepped(b).astype(jnp.bfloat16)
        gram_buf[...] += dot_transposed(part, part) * (1.0 / cols)

    row = lax.broadcasted_iota(jnp.int32, (SEC, SEC), 0)
    col = lax.broadcasted_iota(jnp.int32, (SEC, SEC), 1)

    @pl.loop(0, 2)
    def orthonormalize(step):
        gram = gram_buf[...]
        size = scaling_of(gram)
        scaled = gram / size
        square = dot_fine(scaled, scaled)
        high = dot_fine(0.0625 * square - 0.5625 * scaled, square)
        root = jnp.where(row == col, 2.25, 0.0) - 2.4375 * scaled + 1.6875 * square + high

        @pl.when(step == 0)
        def keep():
            root_buf[...] = root
            factor_buf[...] = jnp.broadcast_to(lax.rsqrt(size), factor_buf.shape)

        product = dot_fine(root, root_buf[...])

        @pl.when(step == 0)
        def second():
            gram_buf[...] = dot_fine(scaled, product)

        @pl.when(step == 1)
        def mix():
            high_buf[...], low_buf[...] = halves(product * (lax.rsqrt(size) * factor_buf[0:1, 0:1]))

    def mixed(value):
        return dot_split((high_buf[...], low_buf[...]), halves(value))

    own_copy.wait()
    own = jnp.concatenate([top_sum[...], low_sum[...]], axis=0)
    next_buf[...] = mixed(scale * own_buf[...].astype(jnp.float32) - 0.5 * own)
    next_copy.start()
    for k in range(slots):
        col_copy(k).wait()

    @pl.loop(0, count)
    def renormalize(k):
        @pl.loop(0, 2)
        def both(side):
            side_buf[side] = mixed(stepped(meta[1 + side * slots + k])).astype(jnp.bfloat16)

        product = dot(side_buf[0], col_buf[k]).astype(jnp.bfloat16)
        out_buf[k] = dot_transposed(product, side_buf[1]) * SEC ** (-0.5)
        out_copy(k).start()

    next_copy.wait()
    for k in range(slots):
        out_copy(k).wait()


def finish(chunk, cols, meta, energy, row_energy, wave_in, own_sums, column_operators, waves, sums, earlier):
    slots = column_operators.shape[0]
    rows, width = wave_in.shape
    hbm = pl.BlockSpec(memory_space=pltpu.HBM)
    vmem = pl.BlockSpec(memory_space=pltpu.VMEM)
    smem = pl.BlockSpec(memory_space=pltpu.SMEM)
    operands = [meta, energy, row_energy, wave_in, *own_sums, column_operators, *waves, *sums, *earlier]
    specs = [smem, smem, vmem, hbm, vmem, vmem] + [hbm] * (len(operands) - 6)
    fixed = len(operands) - len(earlier)
    square = pltpu.VMEM((SEC, SEC), jnp.float32)
    return pl.pallas_call(
        functools.partial(finish_kernel, chunk, slots, cols),
        out_shape=[
            jax.ShapeDtypeStruct((rows, width), jnp.float32),
            jax.ShapeDtypeStruct((slots, rows, SEC), jnp.float32),
        ],
        in_specs=specs,
        out_specs=[hbm, hbm],
        scratch_shapes=[
            pltpu.VMEM((COLUMN_SECTORS, SEC, SEC), jnp.bfloat16),
            pltpu.VMEM((COLUMN_SECTORS, SEC, SEC), jnp.bfloat16),
            pltpu.VMEM((slots, SEC, SEC), jnp.bfloat16),
            pltpu.VMEM((SEC, width), jnp.bfloat16),
            pltpu.VMEM((SEC, width), jnp.float32),
            pltpu.VMEM((slots, SEC, SEC), jnp.float32),
            square,
            square,
            pltpu.VMEM((SEC, SEC), jnp.bfloat16),
            pltpu.VMEM((SEC, SEC), jnp.bfloat16),
            pltpu.VMEM((2, SEC, SEC), jnp.bfloat16),
            pltpu.VMEM((8, 128), jnp.float32),
            pltpu.SemaphoreType.DMA((3, max(slots, COLUMN_SECTORS * HALVES))),
            pltpu.SemaphoreType.DMA((slots,)),
            pltpu.SemaphoreType.DMA((2,)),
        ],
        input_output_aliases={fixed: 0, fixed + 1: 1} if earlier else {},
        cost_estimate=pl.CostEstimate(flops=100 * SEC**3, bytes_accessed=40 * SEC * SEC, transcendentals=0),
        name="finish",
    )(*operands)


LINE = 4
PAIR = 2
SWAP = ((0, 1), (1, 0), (2, 3), (3, 2))
MIDDLE = ((0, 0), (1, 2), (2, 1), (3, 3))


def along_line(value, moves):
    pairs = [(z * PAIR + x, to * PAIR + x) for z, to in moves for x in range(PAIR)]
    return lax.ppermute(value, "ops", pairs)


def across(value):
    return lax.ppermute(value, "ops", [(i, i ^ 1) for i in range(LINE * PAIR)])


def shifted(value, axis, size, shift, unit):
    pairs = [(i, (i // unit + shift) % (size // unit) * unit + i % unit) for i in range(size)]
    return lax.ppermute(value, axis, pairs)


def add(*values):
    total = values[0].astype(jnp.float32)
    for value in values[1:]:
        total = total + value.astype(jnp.float32)
    return total


def add_half(*values):
    return add(*values).astype(jnp.bfloat16)


def swap(value):
    return along_line(value, SWAP)


def middle(value):
    return along_line(value, MIDDLE)


def outward(value):
    return along_line(value, SWAP)


def inward(value):
    return along_line(value, SWAP)


def gather_stream(block, lag, burst, at_middle):
    held, crossed = [block], []
    near, beyond = block, block
    step = 0
    while len(crossed) < LINE:
        sends = {}
        if step == 0:
            sends["near"], sends["beyond"] = (swap, block), (middle, block)
        if step == 1:
            sends["end"], sends["beyond"] = (outward, beyond), (middle, near)
        if step == 2:
            sends["end"] = (outward, beyond)
        first = step - lag
        if first >= 0:
            last = LINE if first >= burst else first + 1
            for index in range(len(crossed), last):
                sends["x" + str(index)] = (across, held[index])
        got = yield sends
        if step == 0:
            near = got["near"]
            held.append(near)
        if step in (1, 2):
            held.append(jnp.where(at_middle, beyond, got["end"]))
        beyond = got.get("beyond")
        crossed += [got[key] for key in sorted(got) if key[0] == "x"]
        step += 1
    return [value for pair in zip(held, crossed) for value in pair]


def scatter_stream(parts, at_middle):
    far = [parts[PAIR * e + 1] for e in range(LINE)]
    near = [parts[PAIR * e] for e in range(LINE)]
    extra, result = [], None
    for blocks in (far, near):
        sends = {"first": (inward, blocks[3])}
        if blocks is near:
            sends["x"] = (across, result.astype(jnp.bfloat16))
        got = yield sends
        if blocks is near:
            extra = [got["x"]]
        result = yield from gathering_steps(blocks, got["first"], at_middle)
    return add(result, *extra)


def gathering_steps(blocks, first, at_middle):
    got = yield {"turn": (middle, add_half(blocks[2], first)), "second": (inward, blocks[2])}
    turn = jnp.where(at_middle, got["turn"].astype(jnp.float32), 0.0)
    got = yield {
        "near": (swap, add_half(blocks[1], turn)),
        "beyond": (middle, add_half(blocks[3], got["second"])),
    }
    return add(blocks[0], got["near"], jnp.where(at_middle, got["beyond"].astype(jnp.float32), 0.0))


def scatter_across_stream(parts, at_middle):
    far = [parts[PAIR * e + 1] for e in range(LINE)]
    near = [parts[PAIR * e] for e in range(LINE)]
    both = {}
    for e in (3, 2, 1):
        got = yield {"x": (across, far[e])}
        both[e] = add_half(near[e], got["x"])
    got = yield {"x": (across, far[0]), "first": (inward, both[3])}
    both[0] = add(near[0], got["x"])
    return (yield from gathering_steps(both, got["first"], at_middle))


def share_stream(value, groups):
    size = LINE * PAIR
    got = yield {d: (lambda v, d=d: shifted(v, "sec", groups, d, 1), value) for d in range(1, groups)}
    value = add(value, *got.values())
    got = yield {1: (across, value)}
    value = add(value, got[1])
    got = yield {d: (lambda v, d=d: shifted(v, "ops", size, d, PAIR), value) for d in range(1, LINE)}
    return add(value, *got.values())


class Rounds:
    def __init__(self, at_middle):
        self.at_middle = at_middle
        self.streams, self.events, self.results = {}, {}, {}

    def add(self, name, turn, stream):
        self.streams[name] = [turn, stream, None]

    def at(self, turn, event):
        self.events[turn] = event

    def run(self, turns):
        history = []
        for turn in range(turns):
            if turn in self.events:
                self.events[turn]()
            sends = []
            for name in list(self.streams):
                due, stream, got = self.streams[name]
                if due != turn:
                    continue
                try:
                    wanted = stream.send(got)
                except StopIteration as end:
                    self.results[name] = end.value
                    del self.streams[name]
                    continue
                sends += [(name, key, move, value) for key, (move, value) in wanted.items()]
                self.streams[name] = [turn + 2, stream, {}]
            earlier = history[turn - 2] if turn >= 2 else []
            values = [value for *_, value in sends]
            if values and earlier:
                values, _ = lax.optimization_barrier((values, earlier))
            ready = [(name, key, move, value) for (name, key, move, _), value in zip(sends, values)]
            out = [send for send in ready if send[2] is outward]
            back = [send for send in ready if send[2] is inward]
            here = []

            def deliver(arrived, *targets):
                here.append(arrived)
                for name, key, *_ in targets:
                    self.streams[name][2][key] = arrived

            for one, two in zip(out, back):
                deliver(swap(jnp.where(self.at_middle, one[3], two[3])), one, two)
            joined = min(len(out), len(back))
            for send in ready:
                if not any(send is other for other in out[:joined] + back[:joined]):
                    deliver(send[2](send[3]), send)
            history.append(here)


def halves_of(value):
    return [value[i * HALF : (i + 1) * HALF] for i in range(value.shape[0] // HALF)]


def on_links(groups, waves_own, table, terms, diagonal, ending):
    place = lax.axis_index("ops")
    z = place // PAIR
    at_middle = jnp.logical_or(z == 1, z == 2)

    def gathered_at(sector):
        away = z ^ (sector // PAIR)
        turned = jnp.logical_and(at_middle, away >= 2)
        return jnp.where(turned, 5 - away, away) * PAIR + ((place ^ sector) & 1)

    def scattered_at(sector):
        return (z ^ (sector // PAIR)) * PAIR + ((place ^ sector) & 1)

    source, target = table
    sum_places = [gathered_at(source), scattered_at(target), gathered_at(target)]
    end_places = [gathered_at(source), gathered_at(target)]
    rounds = Rounds(at_middle)
    kept, energies = {}, {}

    def both(name, chunk):
        return [rounds.results[name + str(chunk) + str(half)] for half in range(HALVES)]

    def start(name, turn, make):
        for half in range(HALVES):
            rounds.add(name + str(half), turn + half, make(half))

    def spread(stream, parts, burst):
        own = yield from stream(parts, at_middle)
        gathered = yield from gather_stream(own.astype(jnp.bfloat16), 2, burst, at_middle)
        return own, gathered

    def sum_terms(chunk, turn, stream, burst):
        def event():
            kept[chunk] = [piece for pair in zip(*both("wave", chunk)) for piece in pair]
            parts, energies[chunk] = terms(chunk, sum_places, kept[chunk])
            start("sum" + str(chunk), turn, lambda half: spread(stream, parts[half::HALVES], burst))

        return event

    def share_energy():
        index = place * groups + lax.axis_index("sec")
        slot = lax.broadcasted_iota(jnp.int32, (8, 128), 0) * 128 + lax.broadcasted_iota(jnp.int32, (8, 128), 1)
        total = diagonal + energies[0] + energies[1]
        rounds.add("energy", 20, share_stream(jnp.where(slot == index, total, 0.0), groups))

    waves = halves_of(waves_own)
    start("wave0", 2, lambda half: gather_stream(waves[half], 0, LINE, at_middle))
    start("wave1", 8, lambda half: gather_stream(waves[HALVES + half], 1, LINE, at_middle))
    rounds.at(12, sum_terms(0, 12, scatter_stream, LINE))
    rounds.at(20, lambda: (sum_terms(1, 20, scatter_across_stream, 1)(), share_energy()))
    rounds.run(48)
    energy = jnp.sum(rounds.results["energy"])
    own, sums = [], []
    for chunk in range(2):
        (top, top_sums), (low, low_sums) = both("sum", chunk)
        own.append([top, low])
        sums.append([piece for pair in zip(top_sums, low_sums) for piece in pair])
    return ending(energy, end_places, own, [kept[0], kept[1]], sums)


def anywhere(chunks, waves_own, table, terms, diagonal, ending):
    source, target = table

    def pieces_of(block):
        return [half for i in range(COLUMN_SECTORS) for half in halves_of(block[:, i * SEC : (i + 1) * SEC])]

    def gather(block):
        return pieces_of(lax.all_gather(block, "ops", axis=1, tiled=True))

    waves, own, energy = [], [], diagonal
    for chunk in range(chunks):
        waves.append(gather(waves_own[chunk * SEC : (chunk + 1) * SEC]))
        parts, part_energy = terms(chunk, [source, target, target], waves[chunk])
        energy = energy + part_energy
        columns = [jnp.concatenate(parts[i * HALVES : (i + 1) * HALVES], axis=0) for i in range(COLUMN_SECTORS)]
        joined = jnp.concatenate(columns, axis=1)
        own.append(lax.psum_scatter(joined, "ops", scatter_dimension=1, tiled=True).astype(jnp.float32))
    sums = [gather(value.astype(jnp.bfloat16)) for value in own]
    own = [halves_of(value) for value in own]
    energy = lax.psum(energy, ("ops", "sec"))
    return ending(energy, [source, target], own, waves, sums)


def on_device(sizes, wave_in, row_energy, row_operators, column_operators, term_count, source, target):
    rows, width = wave_in.shape
    chunks = rows // SEC
    cols = width * sizes["ops"]
    entries = cols * rows * sizes["sec"]

    def table(places):
        return jnp.concatenate([term_count, *places]).astype(jnp.int32)

    def terms(chunk, places, blocks):
        return term_sums(chunk, table(places), row_operators, column_operators, blocks)

    def ending(numerator, places, own, waves, sums):
        energy = numerator / entries
        outs = ()
        for i in range(chunks):
            outs = finish(
                i, cols, table(places), energy[None], row_energy[:, None], wave_in, own[i],
                column_operators, waves[i], sums[i], outs,
            )
        return (outs[0], outs[1], energy)

    amplitude = wave_in.astype(jnp.float32)
    diagonal = jnp.sum(row_energy[:, None] * amplitude * amplitude)
    planned = sizes["ops"] == LINE * PAIR == COLUMN_SECTORS and width == SEC and chunks == 2
    if planned:
        return on_links(sizes["sec"], wave_in, (source, target), terms, diagonal, ending)
    return anywhere(chunks, wave_in, (source, target), terms, diagonal, ending)


def solution(mesh):
    placed = (
        P("sec", "ops"),
        P("sec"),
        P("ops", "sec", None),
        P("ops", None, None),
        P("ops"),
        P("ops"),
        P("ops"),
    )
    return jax.shard_map(
        functools.partial(on_device, dict(mesh.shape)),
        mesh=mesh,
        in_specs=placed,
        out_specs=(P("sec", "ops"), P("ops", "sec", None), P()),
        check_vma=False,
    )
```

```python
import functools

import jax
import jax.numpy as jnp
from jax import lax
from jax.experimental import pallas as pl
from jax.experimental.pallas import tpu as pltpu
from jax.sharding import PartitionSpec as P

SEC = 512
COLUMN_SECTORS = 8
HALVES = 2
HALF = SEC // HALVES


def halves(value):
    high = value.astype(jnp.bfloat16)
    return high, (value - high.astype(jnp.float32)).astype(jnp.bfloat16)


def dot(first, second):
    return jnp.dot(first, second, preferred_element_type=jnp.float32)


def dot_transposed(first, second):
    return lax.dot_general(
        first, second, (((1,), (1,)), ((), ())), preferred_element_type=jnp.float32
    )


def dot_split(first, second):
    (first_high, first_low), (second_high, second_low) = first, second
    return dot(first_high, second_high) + (dot(first_high, second_low) + dot(first_low, second_high))


def dot_fine(first, second):
    return dot_split(halves(first), halves(second))


def term_kernel(chunk, slots, meta, rows_hbm, cols_hbm, *refs):
    count = meta[0]
    pieces = COLUMN_SECTORS * HALVES
    blocks, outs = refs[:pieces], refs[pieces : 2 * pieces]
    energy_out, row_buf, col_buf, wave_buf, target_buf, total, sems = refs[2 * pieces :]

    def row_copy(k):
        part = rows_hbm.at[k, pl.ds(chunk * SEC, SEC)]
        return pltpu.make_async_copy(part, row_buf.at[k], sems.at[0, k])

    def col_copy(k):
        return pltpu.make_async_copy(cols_hbm.at[k], col_buf.at[k], sems.at[1, k])

    def wave_copy(k, piece, half):
        return pltpu.make_async_copy(blocks[piece], wave_buf.at[k, pl.ds(half * HALF, HALF)], sems.at[2 + half, k])

    def target_copy(k, piece, half):
        return pltpu.make_async_copy(blocks[piece], target_buf.at[k, pl.ds(half * HALF, HALF)], sems.at[2 + HALVES + half, k])

    @pl.loop(0, count)
    def start(k):
        row_copy(k).start()
        for index in range(COLUMN_SECTORS):

            @pl.when(meta[1 + k] == index)
            def fetch(index=index):
                for half in range(HALVES):
                    wave_copy(k, index * HALVES + half, half).start()

        col_copy(k).start()
        for index in range(COLUMN_SECTORS):

            @pl.when(meta[1 + 2 * slots + k] == index)
            def fetch_target(index=index):
                for half in range(HALVES):
                    target_copy(k, index * HALVES + half, half).start()

    total[...] = jnp.zeros_like(total)
    energy_out[...] = jnp.zeros_like(energy_out)

    @pl.loop(0, count)
    def compute(k):
        row_copy(k).wait()
        for half in range(HALVES):
            wave_copy(k, half, half).wait()
        inner = dot(row_buf[k], wave_buf[k]).astype(jnp.bfloat16)
        col_copy(k).wait()
        place = meta[1 + slots + k]
        contribution = dot(inner, col_buf[k])
        total[place] = total[place] + contribution
        for half in range(HALVES):
            target_copy(k, half, half).wait()
        overlap = target_buf[k].astype(jnp.float32) * contribution
        energy_out[...] += jnp.sum(overlap, axis=0, keepdims=True)

    for index in range(COLUMN_SECTORS):
        for half in range(HALVES):
            outs[index * HALVES + half][...] = total[index, pl.ds(half * HALF, HALF)].astype(jnp.bfloat16)


def term_sums(chunk, meta, row_operators, column_operators, blocks):
    slots = row_operators.shape[0]
    hbm = pl.BlockSpec(memory_space=pltpu.HBM)
    vmem = pl.BlockSpec(memory_space=pltpu.VMEM)
    pieces = COLUMN_SECTORS * HALVES
    buffer = pltpu.VMEM((slots, SEC, SEC), jnp.bfloat16)
    *parts, energy = pl.pallas_call(
        functools.partial(term_kernel, chunk, slots),
        out_shape=[jax.ShapeDtypeStruct((HALF, SEC), jnp.bfloat16)] * pieces
        + [jax.ShapeDtypeStruct((1, SEC), jnp.float32)],
        in_specs=[pl.BlockSpec(memory_space=pltpu.SMEM)] + [hbm] * (2 + pieces),
        out_specs=[vmem] * (pieces + 1),
        scratch_shapes=[
            buffer,
            buffer,
            buffer,
            buffer,
            pltpu.VMEM((COLUMN_SECTORS, SEC, SEC), jnp.float32),
            pltpu.SemaphoreType.DMA((2 + 2 * HALVES, slots)),
        ],
        cost_estimate=pl.CostEstimate(flops=8 * SEC**3, bytes_accessed=14 * SEC * SEC, transcendentals=0),
        name="term_sums",
    )(meta, row_operators, column_operators, *blocks)
    return parts, jnp.sum(energy)


def scaling_of(gram):
    return jnp.sqrt(jnp.sum(gram * gram, keepdims=True) + 1e-6)


def finish_kernel(chunk, slots, cols, meta, energy, row_energy, wave_hbm, top_sum, low_sum, cols_hbm, *refs):
    count = meta[0]
    pieces = COLUMN_SECTORS * HALVES
    waves, sums = refs[:pieces], refs[pieces : 2 * pieces]
    rest = refs[2 * pieces :]
    if chunk:
        rest = rest[2:]
    next_hbm, table_hbm, wave_buf, sum_buf, col_buf, own_buf, next_buf, out_buf = rest[:8]
    gram_buf, root_buf, high_buf, low_buf, half_buf, factor_buf, sems, out_sems, own_sems = rest[8:]
    span = pl.ds(chunk * SEC, SEC)

    def piece_copies(b, source):
        copies = []
        for half in range(HALVES):
            index, part = source * HALVES + half, pl.ds(half * HALF, HALF)
            place = b * HALVES + half
            copies.append(pltpu.make_async_copy(waves[index], wave_buf.at[b, part], sems.at[0, place]))
            copies.append(pltpu.make_async_copy(sums[index], sum_buf.at[b, part], sems.at[1, place]))
        return copies

    def col_copy(k):
        return pltpu.make_async_copy(cols_hbm.at[k], col_buf.at[k], sems.at[2, k])

    def out_copy(k):
        return pltpu.make_async_copy(out_buf.at[k], table_hbm.at[k, span], out_sems.at[k])

    own_copy = pltpu.make_async_copy(wave_hbm.at[span], own_buf, own_sems.at[0])
    next_copy = pltpu.make_async_copy(next_buf, next_hbm.at[span], own_sems.at[1])

    for b in range(COLUMN_SECTORS):
        for copy in piece_copies(b, b):
            copy.start()
    own_copy.start()
    for k in range(slots):
        col_copy(k).start()
    scale = 1.0 + 0.5 * energy[0] - 0.5 * row_energy[span, :]

    @pl.loop(count, slots)
    def clear(k):
        out_buf[k] = jnp.zeros((SEC, SEC), jnp.float32)
        out_copy(k).start()

    def stepped(b):
        return scale * wave_buf[b].astype(jnp.float32) - 0.5 * sum_buf[b].astype(jnp.float32)

    gram_buf[...] = jnp.zeros_like(gram_buf)

    @pl.loop(0, COLUMN_SECTORS // 2)
    def accumulate(pair):
        part = []
        for b in (2 * pair, 2 * pair + 1):
            for copy in piece_copies(b, 0):
                copy.wait()
            part.append(stepped(b).astype(jnp.bfloat16))
        part = jnp.concatenate(part, axis=1)
        gram_buf[...] += dot_transposed(part, part)

    row = lax.broadcasted_iota(jnp.int32, (SEC, SEC), 0)
    col = lax.broadcasted_iota(jnp.int32, (SEC, SEC), 1)

    @pl.loop(0, 2)
    def orthonormalize(step):
        gram = gram_buf[...] * jnp.where(step == 0, 1.0 / cols, 1.0)
        size = scaling_of(gram)
        scaled = gram * (1.0 / size)
        split = halves(scaled)
        square = dot_split(split, split)
        high = dot_fine(0.0625 * square - 0.5625 * scaled, square)
        root = jnp.where(row == col, 2.25, 0.0) - 2.4375 * scaled + 1.6875 * square + high

        @pl.when(step == 0)
        def keep():
            root_buf[...] = root
            factor_buf[...] = jnp.broadcast_to(lax.rsqrt(size), factor_buf.shape)

        product = dot_fine(root, root_buf[...])

        @pl.when(step == 0)
        def second():
            gram_buf[...] = dot_split(split, halves(product))

        @pl.when(step == 1)
        def mix():
            high_buf[...], low_buf[...] = halves(product * (lax.rsqrt(size) * factor_buf[0:1, 0:1]))

    def mixed(value):
        return dot_split((high_buf[...], low_buf[...]), halves(value))

    own_copy.wait()
    own = jnp.concatenate([top_sum[...], low_sum[...]], axis=0)
    next_buf[...] = mixed(scale * own_buf[...].astype(jnp.float32) - 0.5 * own)
    next_copy.start()
    for k in range(slots):
        col_copy(k).wait()

    @pl.loop(0, COLUMN_SECTORS)
    def round_sector(b):
        wanted = False
        for k in range(slots):
            named = jnp.logical_or(meta[1 + k] == b, meta[1 + slots + k] == b)
            wanted = jnp.logical_or(wanted, jnp.logical_and(k < count, named))

        @pl.when(wanted)
        def form():
            half_buf[b] = mixed(stepped(b)).astype(jnp.bfloat16)

    @pl.loop(0, count)
    def renormalize(k):
        product = dot(half_buf[meta[1 + k]], col_buf[k]).astype(jnp.bfloat16)
        out_buf[k] = dot_transposed(product, half_buf[meta[1 + slots + k]]) * SEC ** (-0.5)
        out_copy(k).start()

    next_copy.wait()
    for k in range(slots):
        out_copy(k).wait()


def finish(chunk, cols, meta, energy, row_energy, wave_in, own_sums, column_operators, waves, sums, earlier):
    slots = column_operators.shape[0]
    rows, width = wave_in.shape
    hbm = pl.BlockSpec(memory_space=pltpu.HBM)
    vmem = pl.BlockSpec(memory_space=pltpu.VMEM)
    smem = pl.BlockSpec(memory_space=pltpu.SMEM)
    operands = [meta, energy, row_energy, wave_in, *own_sums, column_operators, *waves, *sums, *earlier]
    specs = [smem, smem, vmem, hbm, vmem, vmem] + [hbm] * (len(operands) - 6)
    fixed = len(operands) - len(earlier)
    square = pltpu.VMEM((SEC, SEC), jnp.float32)
    return pl.pallas_call(
        functools.partial(finish_kernel, chunk, slots, cols),
        out_shape=[
            jax.ShapeDtypeStruct((rows, width), jnp.float32),
            jax.ShapeDtypeStruct((slots, rows, SEC), jnp.float32),
        ],
        in_specs=specs,
        out_specs=[hbm, hbm],
        scratch_shapes=[
            pltpu.VMEM((COLUMN_SECTORS, SEC, SEC), jnp.bfloat16),
            pltpu.VMEM((COLUMN_SECTORS, SEC, SEC), jnp.bfloat16),
            pltpu.VMEM((slots, SEC, SEC), jnp.bfloat16),
            pltpu.VMEM((SEC, width), jnp.bfloat16),
            pltpu.VMEM((SEC, width), jnp.float32),
            pltpu.VMEM((slots, SEC, SEC), jnp.float32),
            square,
            square,
            pltpu.VMEM((SEC, SEC), jnp.bfloat16),
            pltpu.VMEM((SEC, SEC), jnp.bfloat16),
            pltpu.VMEM((COLUMN_SECTORS, SEC, SEC), jnp.bfloat16),
            pltpu.VMEM((8, 128), jnp.float32),
            pltpu.SemaphoreType.DMA((3, max(slots, COLUMN_SECTORS * HALVES))),
            pltpu.SemaphoreType.DMA((slots,)),
            pltpu.SemaphoreType.DMA((2,)),
        ],
        input_output_aliases={fixed: 0, fixed + 1: 1} if earlier else {},
        cost_estimate=pl.CostEstimate(flops=100 * SEC**3, bytes_accessed=40 * SEC * SEC, transcendentals=0),
        name="finish",
    )(*operands)


LINE = 4
PAIR = 2
SWAP = ((0, 1), (1, 0), (2, 3), (3, 2))


def along_line(value, moves):
    pairs = [(z * PAIR + x, to * PAIR + x) for z, to in moves for x in range(PAIR)]
    return lax.ppermute(value, "ops", pairs)


def across(value):
    return lax.ppermute(value, "ops", [(i, i ^ 1) for i in range(LINE * PAIR)])


def shifted(value, axis, size, shift, unit):
    pairs = [(i, (i // unit + shift) % (size // unit) * unit + i % unit) for i in range(size)]
    return lax.ppermute(value, axis, pairs)


def add(*values):
    total = values[0].astype(jnp.float32)
    for value in values[1:]:
        total = total + value.astype(jnp.float32)
    return total


def add_half(*values):
    return add(*values).astype(jnp.bfloat16)


def swap(value):
    return along_line(value, SWAP)


def middle(value):
    groups = lax.axis_size("sec")
    pairs = []
    for z in range(LINE):
        for x in range(PAIR):
            for group in range(groups):
                to = (LINE - 1 - z, group) if z in (1, 2) else (z, group ^ 1)
                pairs.append(((z * PAIR + x) * groups + group, (to[0] * PAIR + x) * groups + to[1]))
    return lax.ppermute(value, ("ops", "sec"), pairs)


def outward(value):
    return along_line(value, SWAP)


def inward(value):
    return along_line(value, SWAP)


def gather_stream(block, lag, burst, at_middle):
    held, crossed = [block], []
    near, beyond = block, block
    step = 0
    while len(crossed) < LINE:
        sends = {}
        if step == 0:
            sends["near"], sends["beyond"] = (swap, block), (middle, block)
        if step == 1:
            sends["end"], sends["beyond"] = (outward, beyond), (middle, near)
        if step == 2:
            sends["end"] = (outward, beyond)
        first = step - lag
        if first >= 0:
            last = LINE if first >= burst else first + 1
            for index in range(len(crossed), last):
                sends["x" + str(index)] = (across, held[index])
        got = yield sends
        if step == 0:
            near = got["near"]
            held.append(near)
        if step in (1, 2):
            held.append(jnp.where(at_middle, beyond, got["end"]))
        beyond = got.get("beyond")
        crossed += [got[key] for key in sorted(got) if key[0] == "x"]
        step += 1
    return [value for pair in zip(held, crossed) for value in pair]


def scatter_stream(parts, at_middle):
    far = [parts[PAIR * e + 1] for e in range(LINE)]
    near = [parts[PAIR * e] for e in range(LINE)]
    extra, result = [], None
    for blocks in (far, near):
        sends = {"first": (inward, blocks[3])}
        if blocks is near:
            sends["x"] = (across, result.astype(jnp.bfloat16))
        got = yield sends
        if blocks is near:
            extra = [got["x"]]
        result = yield from gathering_steps(blocks, got["first"], at_middle)
    return add(result, *extra)


def gathering_steps(blocks, first, at_middle):
    got = yield {"turn": (middle, add_half(blocks[2], first)), "second": (inward, blocks[2])}
    turn = jnp.where(at_middle, got["turn"].astype(jnp.float32), 0.0)
    got = yield {
        "near": (swap, add_half(blocks[1], turn)),
        "beyond": (middle, add_half(blocks[3], got["second"])),
    }
    return add(blocks[0], got["near"], jnp.where(at_middle, got["beyond"].astype(jnp.float32), 0.0))


def scatter_across_stream(parts, at_middle):
    far = [parts[PAIR * e + 1] for e in range(LINE)]
    near = [parts[PAIR * e] for e in range(LINE)]
    both = {}
    for e in (3, 2, 1):
        got = yield {"x": (across, far[e])}
        both[e] = add_half(near[e], got["x"])
    got = yield {"x": (across, far[0]), "first": (inward, both[3])}
    both[0] = add(near[0], got["x"])
    return (yield from gathering_steps(both, got["first"], at_middle))


def share_stream(value, groups):
    size = LINE * PAIR
    got = yield {d: (lambda v, d=d: shifted(v, "sec", groups, d, 1), value) for d in range(1, groups)}
    value = add(value, *got.values())
    got = yield {1: (across, value)}
    value = add(value, got[1])
    got = yield {d: (lambda v, d=d: shifted(v, "ops", size, d, PAIR), value) for d in range(1, LINE)}
    return add(value, *got.values())


class Rounds:
    def __init__(self, at_middle):
        self.at_middle = at_middle
        self.streams, self.events, self.results = {}, {}, {}

    def add(self, name, turn, stream):
        self.streams[name] = [turn, stream, None]

    def at(self, turn, event):
        self.events[turn] = event

    def run(self, turns):
        history = []
        for turn in range(turns):
            if turn in self.events:
                self.events[turn]()
            sends = []
            for name in list(self.streams):
                due, stream, got = self.streams[name]
                if due != turn:
                    continue
                try:
                    wanted = stream.send(got)
                except StopIteration as end:
                    self.results[name] = end.value
                    del self.streams[name]
                    continue
                sends += [(name, key, move, value) for key, (move, value) in wanted.items()]
                self.streams[name] = [turn + 2, stream, {}]
            earlier = history[turn - 2] if turn >= 2 else []
            values = [value for *_, value in sends]
            if values and earlier:
                values, _ = lax.optimization_barrier((values, earlier))
            ready = [(name, key, move, value) for (name, key, move, _), value in zip(sends, values)]
            out = [send for send in ready if send[2] is outward]
            back = [send for send in ready if send[2] is inward]
            here = []

            def deliver(arrived, *targets):
                here.append(arrived)
                for name, key, *_ in targets:
                    self.streams[name][2][key] = arrived

            for one, two in zip(out, back):
                deliver(swap(jnp.where(self.at_middle, one[3], two[3])), one, two)
            joined = min(len(out), len(back))
            for send in ready:
                if not any(send is other for other in out[:joined] + back[:joined]):
                    deliver(send[2](send[3]), send)
            history.append(here)


def halves_of(value):
    return [value[i * HALF : (i + 1) * HALF] for i in range(value.shape[0] // HALF)]


def on_links(groups, waves_own, table, terms, diagonal, ending):
    place = lax.axis_index("ops")
    z = place // PAIR
    at_middle = jnp.logical_or(z == 1, z == 2)

    def gathered_at(sector):
        away = z ^ (sector // PAIR)
        turned = jnp.logical_and(at_middle, away >= 2)
        return jnp.where(turned, 5 - away, away) * PAIR + ((place ^ sector) & 1)

    def scattered_at(sector):
        return (z ^ (sector // PAIR)) * PAIR + ((place ^ sector) & 1)

    source, target = table
    sum_places = [gathered_at(source), scattered_at(target), gathered_at(target)]
    end_places = [gathered_at(source), gathered_at(target)]
    rounds = Rounds(at_middle)
    kept, energies = {}, {}

    def both(name, chunk):
        return [rounds.results[name + str(chunk) + str(half)] for half in range(HALVES)]

    def start(name, turn, make):
        for half in range(HALVES):
            rounds.add(name + str(half), turn + half, make(half))

    def spread(stream, parts, burst):
        own = yield from stream(parts, at_middle)
        gathered = yield from gather_stream(own.astype(jnp.bfloat16), 2, burst, at_middle)
        return own, gathered

    def sum_terms(chunk, turn, stream, burst):
        def event():
            kept[chunk] = [piece for pair in zip(*both("wave", chunk)) for piece in pair]
            parts, energies[chunk] = terms(chunk, sum_places, kept[chunk])
            start("sum" + str(chunk), turn, lambda half: spread(stream, parts[half::HALVES], burst))

        return event

    def share_energy():
        index = place * groups + lax.axis_index("sec")
        slot = lax.broadcasted_iota(jnp.int32, (8, 128), 0) * 128 + lax.broadcasted_iota(jnp.int32, (8, 128), 1)
        total = diagonal + energies[0] + energies[1]
        rounds.add("energy", 20, share_stream(jnp.where(slot == index, total, 0.0), groups))

    waves = halves_of(waves_own)
    start("wave0", 2, lambda half: gather_stream(waves[half], 0, LINE, at_middle))
    start("wave1", 8, lambda half: gather_stream(waves[HALVES + half], 1, LINE, at_middle))
    rounds.at(12, sum_terms(0, 12, scatter_stream, LINE))
    rounds.at(20, lambda: (sum_terms(1, 20, scatter_across_stream, 1)(), share_energy()))
    rounds.run(48)
    energy = jnp.sum(rounds.results["energy"])
    own, sums = [], []
    for chunk in range(2):
        (top, top_sums), (low, low_sums) = both("sum", chunk)
        own.append([top, low])
        sums.append([piece for pair in zip(top_sums, low_sums) for piece in pair])
    return ending(energy, end_places, own, [kept[0], kept[1]], sums)


def anywhere(chunks, waves_own, table, terms, diagonal, ending):
    source, target = table

    def pieces_of(block):
        return [half for i in range(COLUMN_SECTORS) for half in halves_of(block[:, i * SEC : (i + 1) * SEC])]

    def gather(block):
        return pieces_of(lax.all_gather(block, "ops", axis=1, tiled=True))

    waves, own, energy = [], [], diagonal
    for chunk in range(chunks):
        waves.append(gather(waves_own[chunk * SEC : (chunk + 1) * SEC]))
        parts, part_energy = terms(chunk, [source, target, target], waves[chunk])
        energy = energy + part_energy
        columns = [jnp.concatenate(parts[i * HALVES : (i + 1) * HALVES], axis=0) for i in range(COLUMN_SECTORS)]
        joined = jnp.concatenate(columns, axis=1)
        own.append(lax.psum_scatter(joined, "ops", scatter_dimension=1, tiled=True).astype(jnp.float32))
    sums = [gather(value.astype(jnp.bfloat16)) for value in own]
    own = [halves_of(value) for value in own]
    energy = lax.psum(energy, ("ops", "sec"))
    return ending(energy, [source, target], own, waves, sums)


def on_device(sizes, wave_in, row_energy, row_operators, column_operators, term_count, source, target):
    rows, width = wave_in.shape
    chunks = rows // SEC
    cols = width * sizes["ops"]
    entries = cols * rows * sizes["sec"]

    def table(places):
        return jnp.concatenate([term_count, *places]).astype(jnp.int32)

    def terms(chunk, places, blocks):
        return term_sums(chunk, table(places), row_operators, column_operators, blocks)

    def ending(numerator, places, own, waves, sums):
        energy = numerator / entries
        outs = ()
        for i in range(chunks):
            outs = finish(
                i, cols, table(places), energy[None], row_energy[:, None], wave_in, own[i],
                column_operators, waves[i], sums[i], outs,
            )
        return (outs[0], outs[1], energy)

    amplitude = wave_in.astype(jnp.float32)
    diagonal = jnp.sum(row_energy[:, None] * amplitude * amplitude)
    planned = sizes["ops"] == LINE * PAIR == COLUMN_SECTORS and width == SEC and chunks == 2 and sizes["sec"] % 2 == 0
    if planned:
        return on_links(sizes["sec"], wave_in, (source, target), terms, diagonal, ending)
    return anywhere(chunks, wave_in, (source, target), terms, diagonal, ending)


def solution(mesh):
    placed = (
        P("sec", "ops"),
        P("sec"),
        P("ops", "sec", None),
        P("ops", None, None),
        P("ops"),
        P("ops"),
        P("ops"),
    )
    return jax.shard_map(
        functools.partial(on_device, dict(mesh.shape)),
        mesh=mesh,
        in_specs=placed,
        out_specs=(P("sec", "ops"), P("ops", "sec", None), P()),
        check_vma=False,
    )
```

```python
import functools

import jax
import jax.numpy as jnp
from jax import lax
from jax.experimental import pallas as pl
from jax.experimental.pallas import tpu as pltpu
from jax.sharding import PartitionSpec as P

SEC = 512
COLUMN_SECTORS = 8
HALVES = 2
HALF = SEC // HALVES


def halves(value):
    high = value.astype(jnp.bfloat16)
    return high, (value - high.astype(jnp.float32)).astype(jnp.bfloat16)


def dot(first, second):
    return jnp.dot(first, second, preferred_element_type=jnp.float32)


def dot_transposed(first, second):
    return lax.dot_general(
        first, second, (((1,), (1,)), ((), ())), preferred_element_type=jnp.float32
    )


def dot_split(first, second):
    (first_high, first_low), (second_high, second_low) = first, second
    return dot(first_high, second_high) + (dot(first_high, second_low) + dot(first_low, second_high))


def dot_fine(first, second):
    return dot_split(halves(first), halves(second))


def term_kernel(chunk, slots, meta, rows_hbm, cols_hbm, *refs):
    count = meta[0]
    pieces = COLUMN_SECTORS * HALVES
    blocks, outs = refs[:pieces], refs[pieces : 2 * pieces]
    energy_out, row_buf, col_buf, wave_buf, target_buf, total, sems = refs[2 * pieces :]

    def row_copy(k):
        part = rows_hbm.at[k, pl.ds(chunk * SEC, SEC)]
        return pltpu.make_async_copy(part, row_buf.at[k], sems.at[0, k])

    def col_copy(k):
        return pltpu.make_async_copy(cols_hbm.at[k], col_buf.at[k], sems.at[1, k])

    def wave_copy(k, piece, half):
        return pltpu.make_async_copy(blocks[piece], wave_buf.at[k, pl.ds(half * HALF, HALF)], sems.at[2 + half, k])

    def target_copy(k, piece, half):
        return pltpu.make_async_copy(blocks[piece], target_buf.at[k, pl.ds(half * HALF, HALF)], sems.at[2 + HALVES + half, k])

    @pl.loop(0, count)
    def start(k):
        row_copy(k).start()
        for index in range(COLUMN_SECTORS):

            @pl.when(meta[1 + k] == index)
            def fetch(index=index):
                for half in range(HALVES):
                    wave_copy(k, index * HALVES + half, half).start()

        col_copy(k).start()
        for index in range(COLUMN_SECTORS):

            @pl.when(meta[1 + 2 * slots + k] == index)
            def fetch_target(index=index):
                for half in range(HALVES):
                    target_copy(k, index * HALVES + half, half).start()

    total[...] = jnp.zeros_like(total)
    energy_out[...] = jnp.zeros_like(energy_out)

    @pl.loop(0, count)
    def compute(k):
        row_copy(k).wait()
        for half in range(HALVES):
            wave_copy(k, half, half).wait()
        inner = dot(row_buf[k], wave_buf[k]).astype(jnp.bfloat16)
        col_copy(k).wait()
        place = meta[1 + slots + k]
        contribution = dot(inner, col_buf[k])
        total[place] = total[place] + contribution
        for half in range(HALVES):
            target_copy(k, half, half).wait()
        overlap = target_buf[k].astype(jnp.float32) * contribution
        energy_out[...] += jnp.sum(overlap, axis=0, keepdims=True)

    for index in range(COLUMN_SECTORS):
        for half in range(HALVES):
            outs[index * HALVES + half][...] = total[index, pl.ds(half * HALF, HALF)].astype(jnp.bfloat16)


def term_sums(chunk, meta, row_operators, column_operators, blocks):
    slots = row_operators.shape[0]
    hbm = pl.BlockSpec(memory_space=pltpu.HBM)
    vmem = pl.BlockSpec(memory_space=pltpu.VMEM)
    pieces = COLUMN_SECTORS * HALVES
    buffer = pltpu.VMEM((slots, SEC, SEC), jnp.bfloat16)
    *parts, energy = pl.pallas_call(
        functools.partial(term_kernel, chunk, slots),
        out_shape=[jax.ShapeDtypeStruct((HALF, SEC), jnp.bfloat16)] * pieces
        + [jax.ShapeDtypeStruct((1, SEC), jnp.float32)],
        in_specs=[pl.BlockSpec(memory_space=pltpu.SMEM)] + [hbm] * (2 + pieces),
        out_specs=[vmem] * (pieces + 1),
        scratch_shapes=[
            buffer,
            buffer,
            buffer,
            buffer,
            pltpu.VMEM((COLUMN_SECTORS, SEC, SEC), jnp.float32),
            pltpu.SemaphoreType.DMA((2 + 2 * HALVES, slots)),
        ],
        cost_estimate=pl.CostEstimate(flops=8 * SEC**3, bytes_accessed=14 * SEC * SEC, transcendentals=0),
        name="term_sums",
    )(meta, row_operators, column_operators, *blocks)
    return parts, jnp.sum(energy)


def scaling_of(gram):
    return jnp.sqrt(jnp.sum(gram * gram, keepdims=True) + 1e-6)


def finish_kernel(chunk, slots, cols, stages, *refs):
    refs = list(refs)

    def take(number, wanted=True):
        if not wanted:
            return [None] * number
        out = refs[:number]
        del refs[:number]
        return out

    pieces = COLUMN_SECTORS * HALVES
    early, late = 0 in stages, 1 in stages
    (energy, row_energy) = take(2)
    waves, sums = take(pieces), take(pieces)
    high_in, low_in = take(2, not early)
    meta, wave_hbm, top_sum, low_sum, cols_hbm = take(5, late)
    take(2, late and chunk > 0)
    next_hbm, table_hbm = take(2, late)
    high_out, low_out = take(2, not late)
    wave_buf, sum_buf, sems = take(3)
    gram_buf, root_buf, factor_buf = take(3, early)
    high_buf, low_buf = take(2, early and late)
    col_buf, own_buf, next_buf, out_buf, half_buf, out_sems, own_sems = take(7, late)
    high_ref, low_ref = (high_buf, low_buf) if early and late else (high_in, low_in) if late else (high_out, low_out)
    span = pl.ds(chunk * SEC, SEC)

    def piece_copies(b, source):
        copies = []
        for half in range(HALVES):
            index, part = source * HALVES + half, pl.ds(half * HALF, HALF)
            place = b * HALVES + half
            copies.append(pltpu.make_async_copy(waves[index], wave_buf.at[b, part], sems.at[0, place]))
            copies.append(pltpu.make_async_copy(sums[index], sum_buf.at[b, part], sems.at[1, place]))
        return copies

    for b in range(COLUMN_SECTORS):
        for copy in piece_copies(b, b):
            copy.start()
    scale = 1.0 + 0.5 * energy[0] - 0.5 * row_energy[span, :]

    def stepped(b):
        return scale * wave_buf[b].astype(jnp.float32) - 0.5 * sum_buf[b].astype(jnp.float32)

    if late:
        count = meta[0]

        def col_copy(k):
            return pltpu.make_async_copy(cols_hbm.at[k], col_buf.at[k], sems.at[2, k])

        def out_copy(k):
            return pltpu.make_async_copy(out_buf.at[k], table_hbm.at[k, span], out_sems.at[k])

        own_copy = pltpu.make_async_copy(wave_hbm.at[span], own_buf, own_sems.at[0])
        next_copy = pltpu.make_async_copy(next_buf, next_hbm.at[span], own_sems.at[1])
        own_copy.start()
        for k in range(slots):
            col_copy(k).start()

        @pl.loop(count, slots)
        def clear(k):
            out_buf[k] = jnp.zeros((SEC, SEC), jnp.float32)
            out_copy(k).start()

    if early:
        gram_buf[...] = jnp.zeros_like(gram_buf)

        @pl.loop(0, COLUMN_SECTORS // 2)
        def accumulate(pair):
            part = []
            for b in (2 * pair, 2 * pair + 1):
                for copy in piece_copies(b, 0):
                    copy.wait()
                part.append(stepped(b).astype(jnp.bfloat16))
            part = jnp.concatenate(part, axis=1)
            gram_buf[...] += dot_transposed(part, part)

        row = lax.broadcasted_iota(jnp.int32, (SEC, SEC), 0)
        col = lax.broadcasted_iota(jnp.int32, (SEC, SEC), 1)

        @pl.loop(0, 2)
        def orthonormalize(step):
            gram = gram_buf[...] * jnp.where(step == 0, 1.0 / cols, 1.0)
            size = scaling_of(gram)
            scaled = gram * (1.0 / size)
            split = halves(scaled)
            square = dot_split(split, split)
            high = dot_fine(0.0625 * square - 0.5625 * scaled, square)
            root = jnp.where(row == col, 2.25, 0.0) - 2.4375 * scaled + 1.6875 * square + high

            @pl.when(step == 0)
            def keep():
                root_buf[...] = root
                factor_buf[...] = jnp.broadcast_to(lax.rsqrt(size), factor_buf.shape)

            product = dot_fine(root, root_buf[...])

            @pl.when(step == 0)
            def second():
                gram_buf[...] = dot_split(split, halves(product))

            @pl.when(step == 1)
            def mix():
                mixer = product * (lax.rsqrt(size) * factor_buf[0:1, 0:1])
                high_ref[...], low_ref[...] = halves(mixer)

    if late:

        def mixed(value):
            return dot_split((high_ref[...], low_ref[...]), halves(value))

        own_copy.wait()
        own = jnp.concatenate([top_sum[...], low_sum[...]], axis=0)
        next_buf[...] = mixed(scale * own_buf[...].astype(jnp.float32) - 0.5 * own)
        next_copy.start()

        @pl.loop(0, COLUMN_SECTORS)
        def round_sector(b):
            if not early:
                for copy in piece_copies(b, 0):
                    copy.wait()
            wanted = False
            for k in range(slots):
                named = jnp.logical_or(meta[1 + k] == b, meta[1 + slots + k] == b)
                wanted = jnp.logical_or(wanted, jnp.logical_and(k < count, named))

            @pl.when(wanted)
            def form():
                half_buf[b] = mixed(stepped(b)).astype(jnp.bfloat16)

        for k in range(slots):
            col_copy(k).wait()

        @pl.loop(0, count)
        def renormalize(k):
            product = dot(half_buf[meta[1 + k]], col_buf[k]).astype(jnp.bfloat16)
            out_buf[k] = dot_transposed(product, half_buf[meta[1 + slots + k]]) * SEC ** (-0.5)
            out_copy(k).start()

        next_copy.wait()
        for k in range(slots):
            out_copy(k).wait()


def finish(chunk, cols, stages, energy, row_energy, waves, sums, mixer=(), late=(), earlier=()):
    hbm = pl.BlockSpec(memory_space=pltpu.HBM)
    vmem = pl.BlockSpec(memory_space=pltpu.VMEM)
    smem = pl.BlockSpec(memory_space=pltpu.SMEM)
    operands = [energy, row_energy, *waves, *sums, *mixer]
    specs = [smem, vmem] + [hbm] * (len(waves) + len(sums)) + [vmem] * len(mixer)
    square = pltpu.VMEM((SEC, SEC), jnp.float32)
    sectors = pltpu.VMEM((COLUMN_SECTORS, SEC, SEC), jnp.bfloat16)
    rounded = pltpu.VMEM((SEC, SEC), jnp.bfloat16)
    scratch = [sectors, sectors, pltpu.SemaphoreType.DMA((3, COLUMN_SECTORS * HALVES))]
    slots, aliases = 0, {}
    if 0 in stages:
        scratch += [square, square, pltpu.VMEM((8, 128), jnp.float32)]
    if len(stages) == 2:
        scratch += [rounded, rounded]
    if 1 in stages:
        meta, wave_in, own_sums, column_operators = late
        slots = column_operators.shape[0]
        rows, width = wave_in.shape
        operands += [meta, wave_in, *own_sums, column_operators, *earlier]
        specs += [smem, hbm, vmem, vmem, hbm] + [hbm] * len(earlier)
        if earlier:
            aliases = {len(operands) - 2: 0, len(operands) - 1: 1}
        out_shape = [
            jax.ShapeDtypeStruct((rows, width), jnp.float32),
            jax.ShapeDtypeStruct((slots, rows, SEC), jnp.float32),
        ]
        out_specs = [hbm, hbm]
        scratch += [
            pltpu.VMEM((slots, SEC, SEC), jnp.bfloat16),
            pltpu.VMEM((SEC, width), jnp.bfloat16),
            pltpu.VMEM((SEC, width), jnp.float32),
            pltpu.VMEM((slots, SEC, SEC), jnp.float32),
            sectors,
            pltpu.SemaphoreType.DMA((slots,)),
            pltpu.SemaphoreType.DMA((2,)),
        ]
    else:
        out_shape = [jax.ShapeDtypeStruct((SEC, SEC), jnp.bfloat16)] * 2
        out_specs = [vmem, vmem]
    flops = (58 if 0 in stages else 0) + (22 if 1 in stages else 0)
    return pl.pallas_call(
        functools.partial(finish_kernel, chunk, slots, cols, stages),
        out_shape=out_shape,
        in_specs=specs,
        out_specs=out_specs,
        scratch_shapes=scratch,
        input_output_aliases=aliases,
        cost_estimate=pl.CostEstimate(flops=flops * SEC**3, bytes_accessed=40 * SEC * SEC, transcendentals=0),
        name="finish" + "".join(str(stage) for stage in stages),
    )(*operands)


LINE = 4
PAIR = 2
SWAP = ((0, 1), (1, 0), (2, 3), (3, 2))


def along_line(value, moves):
    pairs = [(z * PAIR + x, to * PAIR + x) for z, to in moves for x in range(PAIR)]
    return lax.ppermute(value, "ops", pairs)


def across(value):
    return lax.ppermute(value, "ops", [(i, i ^ 1) for i in range(LINE * PAIR)])


def shifted(value, axis, size, shift, unit):
    pairs = [(i, (i // unit + shift) % (size // unit) * unit + i % unit) for i in range(size)]
    return lax.ppermute(value, axis, pairs)


def add(*values):
    total = values[0].astype(jnp.float32)
    for value in values[1:]:
        total = total + value.astype(jnp.float32)
    return total


def add_half(*values):
    return add(*values).astype(jnp.bfloat16)


def swap(value):
    return along_line(value, SWAP)


def middle(value):
    groups = lax.axis_size("sec")
    pairs = []
    for z in range(LINE):
        for x in range(PAIR):
            for group in range(groups):
                to = (LINE - 1 - z, group) if z in (1, 2) else (z, group ^ 1)
                pairs.append(((z * PAIR + x) * groups + group, (to[0] * PAIR + x) * groups + to[1]))
    return lax.ppermute(value, ("ops", "sec"), pairs)


def outward(value):
    return along_line(value, SWAP)


def inward(value):
    return along_line(value, SWAP)


def gather_stream(block, lag, burst, at_middle):
    held, crossed = [block], []
    near, beyond = block, block
    step = 0
    while len(crossed) < LINE:
        sends = {}
        if step == 0:
            sends["near"], sends["beyond"] = (swap, block), (middle, block)
        if step == 1:
            sends["end"], sends["beyond"] = (outward, beyond), (middle, near)
        if step == 2:
            sends["end"] = (outward, beyond)
        first = step - lag
        if first >= 0:
            last = LINE if first >= burst else first + 1
            for index in range(len(crossed), last):
                sends["x" + str(index)] = (across, held[index])
        got = yield sends
        if step == 0:
            near = got["near"]
            held.append(near)
        if step in (1, 2):
            held.append(jnp.where(at_middle, beyond, got["end"]))
        beyond = got.get("beyond")
        crossed += [got[key] for key in sorted(got) if key[0] == "x"]
        step += 1
    return [value for pair in zip(held, crossed) for value in pair]


def gather_across_stream(block, at_middle):
    got = yield {"x": (across, block), "near": (swap, block), "beyond": (middle, block)}
    held, crossed = [block, got["near"]], [got["x"]]
    beyond = got["beyond"]
    got = yield {"near": (swap, crossed[0]), "beyond": (middle, crossed[0])}
    crossed.append(got["near"])
    past = got["beyond"]
    got = yield {
        "end": (outward, past), "turn": (middle, crossed[1]), "last": (outward, beyond), "back": (middle, held[1]),
    }
    held.append(jnp.where(at_middle, beyond, got["last"]))
    crossed.append(jnp.where(at_middle, past, got["end"]))
    beyond, past = got["back"], got["turn"]
    got = yield {"end": (outward, past), "last": (outward, beyond)}
    held.append(jnp.where(at_middle, beyond, got["last"]))
    crossed.append(jnp.where(at_middle, past, got["end"]))
    return [value for pair in zip(held, crossed) for value in pair]


def scatter_stream(parts, at_middle):
    far = [parts[PAIR * e + 1] for e in range(LINE)]
    near = [parts[PAIR * e] for e in range(LINE)]
    extra, result = [], None
    for blocks in (far, near):
        sends = {"first": (inward, blocks[3])}
        if blocks is near:
            sends["x"] = (across, result.astype(jnp.bfloat16))
        got = yield sends
        if blocks is near:
            extra = [got["x"]]
        result = yield from gathering_steps(blocks, got["first"], at_middle)
    return add(result, *extra)


def gathering_steps(blocks, first, at_middle):
    got = yield {"turn": (middle, add_half(blocks[2], first)), "second": (inward, blocks[2])}
    turn = jnp.where(at_middle, got["turn"].astype(jnp.float32), 0.0)
    got = yield {
        "near": (swap, add_half(blocks[1], turn)),
        "beyond": (middle, add_half(blocks[3], got["second"])),
    }
    return add(blocks[0], got["near"], jnp.where(at_middle, got["beyond"].astype(jnp.float32), 0.0))


def scatter_across_stream(parts, at_middle):
    far = [parts[PAIR * e + 1] for e in range(LINE)]
    near = [parts[PAIR * e] for e in range(LINE)]
    both = {}
    for e in (3, 2, 1):
        got = yield {"x": (across, far[e])}
        both[e] = add_half(near[e], got["x"])
    got = yield {"x": (across, far[0]), "first": (inward, both[3])}
    both[0] = add(near[0], got["x"])
    return (yield from gathering_steps(both, got["first"], at_middle))


def share_stream(value, groups):
    size = LINE * PAIR
    got = yield {d: (lambda v, d=d: shifted(v, "sec", groups, d, 1), value) for d in range(1, groups)}
    value = add(value, *got.values())
    got = yield {1: (across, value)}
    value = add(value, got[1])
    got = yield {d: (lambda v, d=d: shifted(v, "ops", size, d, PAIR), value) for d in range(1, LINE)}
    return add(value, *got.values())


class Rounds:
    def __init__(self, at_middle):
        self.at_middle = at_middle
        self.streams, self.events, self.results = {}, {}, {}

    def add(self, name, turn, stream):
        self.streams[name] = [turn, stream, None]

    def at(self, turn, event):
        self.events[turn] = event

    def run(self, turns):
        history = []
        for turn in range(turns):
            if turn in self.events:
                self.events[turn]()
            sends = []
            for name in list(self.streams):
                due, stream, got = self.streams[name]
                if due != turn:
                    continue
                try:
                    wanted = stream.send(got)
                except StopIteration as end:
                    self.results[name] = end.value
                    del self.streams[name]
                    continue
                sends += [(name, key, move, value) for key, (move, value) in wanted.items()]
                self.streams[name] = [turn + 2, stream, {}]
            earlier = history[turn - 2] if turn >= 2 else []
            values = [value for *_, value in sends]
            if values and earlier:
                values, _ = lax.optimization_barrier((values, earlier))
            ready = [(name, key, move, value) for (name, key, move, _), value in zip(sends, values)]
            out = [send for send in ready if send[2] is outward]
            back = [send for send in ready if send[2] is inward]
            here = []

            def deliver(arrived, *targets):
                here.append(arrived)
                for name, key, *_ in targets:
                    self.streams[name][2][key] = arrived

            for one, two in zip(out, back):
                deliver(swap(jnp.where(self.at_middle, one[3], two[3])), one, two)
            joined = min(len(out), len(back))
            for send in ready:
                if not any(send is other for other in out[:joined] + back[:joined]):
                    deliver(send[2](send[3]), send)
            history.append(here)


def halves_of(value):
    return [value[i * HALF : (i + 1) * HALF] for i in range(value.shape[0] // HALF)]


def on_links(groups, waves_own, table, terms, diagonal, ending):
    place = lax.axis_index("ops")
    z = place // PAIR
    at_middle = jnp.logical_or(z == 1, z == 2)

    def gathered_at(sector):
        away = z ^ (sector // PAIR)
        turned = jnp.logical_and(at_middle, away >= 2)
        return jnp.where(turned, 5 - away, away) * PAIR + ((place ^ sector) & 1)

    def scattered_at(sector):
        return (z ^ (sector // PAIR)) * PAIR + ((place ^ sector) & 1)

    source, target = table
    sum_places = [gathered_at(source), scattered_at(target), gathered_at(target)]
    end_places = [gathered_at(source), gathered_at(target)]
    rounds = Rounds(at_middle)
    kept, energies = {}, {}

    def both(name, chunk):
        return [rounds.results[name + str(chunk) + str(half)] for half in range(HALVES)]

    def start(name, turn, make):
        for half in range(HALVES):
            rounds.add(name + str(half), turn + half, make(half))

    def spread(stream, parts, gather):
        own = yield from stream(parts, at_middle)
        gathered = yield from gather(own.astype(jnp.bfloat16))
        return own, gathered

    def along_first(lag, burst):
        return lambda block: gather_stream(block, lag, burst, at_middle)

    def across_first(block):
        return gather_across_stream(block, at_middle)

    def sum_terms(chunk, turn, stream, gathers):
        def event():
            kept[chunk] = [piece for pair in zip(*both("wave", chunk)) for piece in pair]
            parts, energies[chunk] = terms(chunk, sum_places, kept[chunk])
            start("sum" + str(chunk), turn, lambda half: spread(stream, parts[half::HALVES], gathers[half]))

        return event

    def share_energy():
        index = place * groups + lax.axis_index("sec")
        slot = lax.broadcasted_iota(jnp.int32, (8, 128), 0) * 128 + lax.broadcasted_iota(jnp.int32, (8, 128), 1)
        total = diagonal + energies[0] + energies[1]
        rounds.add("energy", 20, share_stream(jnp.where(slot == index, total, 0.0), groups))

    waves = halves_of(waves_own)
    start("wave0", 2, lambda half: gather_stream(waves[half], 0, LINE, at_middle))
    start("wave1", 8, lambda half: gather_stream(waves[HALVES + half], 1, LINE, at_middle))
    rounds.at(12, sum_terms(0, 12, scatter_stream, [along_first(2, LINE)] * 2))
    last = [along_first(1, 2), across_first]
    rounds.at(20, lambda: (sum_terms(1, 20, scatter_across_stream, last)(), share_energy()))
    rounds.run(48)
    energy = jnp.sum(rounds.results["energy"])
    own, sums = [], []
    for chunk in range(2):
        (top, top_sums), (low, low_sums) = both("sum", chunk)
        own.append([top, low])
        sums.append([piece for pair in zip(top_sums, low_sums) for piece in pair])
    return ending(energy, end_places, own, [kept[0], kept[1]], sums)


def anywhere(chunks, waves_own, table, terms, diagonal, ending):
    source, target = table

    def pieces_of(block):
        return [half for i in range(COLUMN_SECTORS) for half in halves_of(block[:, i * SEC : (i + 1) * SEC])]

    def gather(block):
        return pieces_of(lax.all_gather(block, "ops", axis=1, tiled=True))

    waves, own, energy = [], [], diagonal
    for chunk in range(chunks):
        waves.append(gather(waves_own[chunk * SEC : (chunk + 1) * SEC]))
        parts, part_energy = terms(chunk, [source, target, target], waves[chunk])
        energy = energy + part_energy
        columns = [jnp.concatenate(parts[i * HALVES : (i + 1) * HALVES], axis=0) for i in range(COLUMN_SECTORS)]
        joined = jnp.concatenate(columns, axis=1)
        own.append(lax.psum_scatter(joined, "ops", scatter_dimension=1, tiled=True).astype(jnp.float32))
    sums = [gather(value.astype(jnp.bfloat16)) for value in own]
    own = [halves_of(value) for value in own]
    energy = lax.psum(energy, ("ops", "sec"))
    return ending(energy, [source, target], own, waves, sums)


def on_device(sizes, wave_in, row_energy, row_operators, column_operators, term_count, source, target):
    rows, width = wave_in.shape
    chunks = rows // SEC
    cols = width * sizes["ops"]
    entries = cols * rows * sizes["sec"]

    def table(places):
        return jnp.concatenate([term_count, *places]).astype(jnp.int32)

    def terms(chunk, places, blocks):
        return term_sums(chunk, table(places), row_operators, column_operators, blocks)

    def ending(numerator, places, own, waves, sums):
        energy = numerator / entries
        outs, heights = (), row_energy[:, None]
        for i in range(chunks):
            late = (table(places), wave_in, own[i], column_operators)
            mixer, stages = (), (0, 1)
            if i < chunks - 1:
                mixer, stages = finish(i, cols, (0,), energy[None], heights, waves[i], sums[i]), (1,)
            outs = finish(i, cols, stages, energy[None], heights, waves[i], sums[i], mixer, late, outs)
        return (outs[0], outs[1], energy)

    amplitude = wave_in.astype(jnp.float32)
    diagonal = jnp.sum(row_energy[:, None] * amplitude * amplitude)
    planned = sizes["ops"] == LINE * PAIR == COLUMN_SECTORS and width == SEC and chunks == 2 and sizes["sec"] % 2 == 0
    if planned:
        return on_links(sizes["sec"], wave_in, (source, target), terms, diagonal, ending)
    return anywhere(chunks, wave_in, (source, target), terms, diagonal, ending)


def solution(mesh):
    placed = (
        P("sec", "ops"),
        P("sec"),
        P("ops", "sec", None),
        P("ops", None, None),
        P("ops"),
        P("ops"),
        P("ops"),
    )
    return jax.shard_map(
        functools.partial(on_device, dict(mesh.shape)),
        mesh=mesh,
        in_specs=placed,
        out_specs=(P("sec", "ops"), P("ops", "sec", None), P()),
        check_vma=False,
    )
```
